32 devices in a mesh: dp: 8 (over z, y), tensor: 4 (over x, core).
Axes of the slice: x: 2, y: 2, z: 4, core: 2. Of those that a mesh axis runs over, the one named last changes fastest.
Arguments:
- tokens: bfloat16 [2048, 768], P('dp'), may hold values from -6 to 6
- segments: int32 [2048], P('dp'), may hold values from -1 to 255, as said below
- first_gain: float32 [768], replicated, may hold values from 0.1 to 1.9
- first_shift: float32 [768], replicated, may hold values from -1.75 to 1.75
- second_gain: float32 [768], replicated, may hold values from 0.1 to 1.9
- second_shift: float32 [768], replicated, may hold values from -1.75 to 1.75
- inlet: bfloat16 [768, 2304], P(None, 'tensor'), may hold values from -1 to 1
- offsets: float32 [12, 192], P('tensor'), may hold values from -3 to 3
- outlet: bfloat16 [768, 768], P('tensor'), may hold values from -1.25 to 1.25
- outlet_bias: float32 [768], replicated, may hold values from -1.75 to 1.75
- expand: bfloat16 [768, 3072], P(None, 'tensor'), may hold values from -0.21875 to 0.21875
- thresholds: float32 [3072], P('tensor'), may hold values from -3 to 3
- contract: bfloat16 [3072, 768], P('tensor'), may hold values from -0.109375 to 0.109375
- contract_bias: float32 [768], replicated, may hold values from -1.75 to 1.75
- cotangent: bfloat16 [2048, 768], P('dp'), may hold values from -6 to 6
Outputs:
- mixed: bfloat16 [2048, 768], P('dp')
- input_grad: bfloat16 [2048, 768], P('dp')
- inlet_grad: float32 [768, 2304], P('dp', 'tensor')
- offsets_grad: float32 [12, 192], P('tensor', 'dp')
- outlet_grad: float32 [768, 768], P('tensor', 'dp')
- expand_grad: float32 [768, 3072], P('dp', 'tensor')
- thresholds_grad: float32 [4, 768], P('tensor', 'dp')
- contract_grad: float32 [3072, 768], P('tensor', 'dp')
- bias_grad: float32 [768], P('dp')
- norm_grads: float32 [4, 768], P(None, 'dp')
The draws below stay inside these ranges and needn't reach their ends.
Inputs may be any that keep to these rules, and one draw needn't show every extreme that they name: `segments`: within each device's 256 slots the used slots come first; their values start at 0 and rise by one from sequence to sequence; each sequence fills 1 to 128 consecutive slots; unused slots hold -1. Some device uses all its slots and holds a sequence of exactly 128 slots; some device uses half of them; some device uses all its slots as 256 sequences of one slot.
All inputs are finite; a program needn't handle non-finite values.
Results may differ from the reference program's by a relative error of at most 0.0067.
Values may be sent and summed in bfloat16 or wider, within the bound.
No kernel may reach another device: no remote copies, remote signals or barrier semaphores. Data moves between devices by JAX's collectives and lax.ppermute only.
A program may use at most 64 MiB of HBM per device.

```python
import math
import jax
import jax.numpy as jnp
from jax import lax

D = 768
H = 12
HS = 64
ROT = 16
FF = 3072
TOK_DEV = 256
LONGEST = 128
TOKENS = 2048
HU_GROUPS = 4
GROUP_UNITS = 768
N_DP = 8


def draw_segments(key, part):
    streams = jax.random.split(key, 5)
    blocks = TOKENS // TOK_DEV
    index = jnp.arange(blocks, dtype=jnp.int32)
    levels = jax.random.randint(streams[0], (blocks,), 0, 4, dtype=jnp.int32)
    base = jnp.right_shift(jnp.full((blocks,), TOK_DEV, jnp.int32), levels)
    extra = jax.random.randint(streams[1], (blocks,), 0, 1 << 20, dtype=jnp.int32) % (base // 2 + 1)
    used = jnp.minimum(base + extra, TOK_DEV)
    fullest = jax.random.randint(streams[2], (), 0, blocks, dtype=jnp.int32)
    singles = (fullest + 2) % blocks
    used = jnp.where(index == fullest, TOK_DEV, used)
    used = jnp.where(index == (fullest + 1) % blocks, TOK_DEV // 2, used)
    used = jnp.where(index == singles, TOK_DEV, used)
    lengths = jax.random.randint(streams[3], (blocks, TOK_DEV), 1, LONGEST + 1, dtype=jnp.int32)
    placed = jax.random.randint(streams[4], (), 0, 2, dtype=jnp.int32)
    column = jnp.arange(TOK_DEV, dtype=jnp.int32)
    lengths = jnp.where((index[:, None] == fullest) & (column[None, :] == placed), LONGEST, lengths)
    lengths = jnp.where(index[:, None] == singles, 1, lengths)
    ends = jnp.cumsum(lengths, axis=1).astype(jnp.int32)
    labels = jax.vmap(lambda row: jnp.searchsorted(row, column, side='right'))(ends).astype(jnp.int32)
    labels = jnp.where(column[None, :] < used[:, None], labels, -1)
    return labels.reshape(-1).astype(jnp.int32)


def draw_inlet(key, part):
    streams = jax.random.split(key, 1)
    base = jax.random.truncated_normal(streams[0], -4.0, 4.0, (D, H, 3, HS), jnp.float32) * D ** (-0.5)
    return jnp.clip(base, -1.0, 1.0).reshape(D, H * 3 * HS).astype(jnp.bfloat16)


def strengthened(entries, key, source, target, parts, factor):
    def block_of(position):
        return (jnp.arange(entries.shape[position]) // (entries.shape[position] // parts)).reshape((-1,) + (1,) * (entries.ndim - 1 - position))

    first = jax.random.permutation(key, parts)[block_of(target)]
    second = (block_of(target) + parts // 2) % parts
    return jnp.where((block_of(source) == first) | (block_of(source) == second), factor * entries, entries)


def shard_levels(own_key, shape, cuts, smallest, top_value):
    factor_of, own = 1.0, jax.random.fold_in(own_key, 6)
    for axis_at, blocks in cuts:
        steps = jnp.exp(jax.random.uniform(jax.random.fold_in(own, axis_at), (blocks,), jnp.float32, smallest / len(cuts), top_value / len(cuts)))
        factor_of = factor_of * jnp.repeat(steps, shape[axis_at] // blocks).reshape([-1 if axis == axis_at else 1 for axis in range(len(shape))])
    return factor_of


def bell_draw(stream_key, dims, scale, bound, shards=(), held_as=jnp.bfloat16):
    drawn = jax.random.normal(stream_key, dims, jnp.float32) * scale
    if len(shards) > 0:
        drawn = shard_levels(stream_key, dims, shards, -0.22, 0.18) * drawn
    return jnp.clip(drawn, min=-bound, max=bound).astype(held_as)


def bell_draw_with(key, extent, spread, bound, cuts, heavy, kind=jnp.bfloat16):
    drawn = spread * jax.random.normal(key, extent, jnp.float32)
    if cuts:
        drawn = drawn * shard_levels(key, extent, cuts, -0.22, 0.18)
    return jnp.clip(strengthened(drawn, jax.random.fold_in(key, 3), *heavy), -bound, bound).astype(kind)


def setup_inputs(seed: int = 0) -> dict:
    key_of = jax.random.split(jax.random.key(seed), 16)
    tokens = bell_draw_with(key_of[0], (TOKENS, D), 1.0, 6.0, ((0, 8),), (0, 1, 8, 2.0))
    segments = draw_segments(jax.random.fold_in(key_of[15], 71), 0)
    first_gain = jnp.clip(1.0 + 0.18 * jax.random.normal(key_of[2], (D,), jnp.float32), 0.1, 1.9)
    first_shift = bell_draw(key_of[3], (D,), 0.3, 1.75, (), jnp.float32)
    second_gain = jnp.clip(1.0 + 0.18 * jax.random.normal(key_of[4], (D,), jnp.float32), 0.1, 1.9)
    second_shift = bell_draw(key_of[5], (D,), 0.3, 1.75, (), jnp.float32)
    inlet = draw_inlet(jax.random.fold_in(key_of[15], 71), 0)
    offsets = bell_draw(key_of[7], (H, 3 * HS), 0.5, 3.0, ((0, 4),), jnp.float32)
    outlet = bell_draw(key_of[8], (H * HS, D), (H * HS // 32) ** -0.5, 1.25, ((0, 4),))
    outlet_bias = bell_draw(key_of[9], (D,), 0.3, 1.75, (), jnp.float32)
    expand = bell_draw(key_of[10], (D, FF), D ** -0.5, 0.21875, ((1, 4),))
    thresholds = bell_draw(key_of[11], (FF,), 0.5, 3.0, ((0, 4),), jnp.float32)
    contract = bell_draw(key_of[12], (FF, D), FF ** -0.5, 0.109375, ((0, 4),))
    contract_bias = bell_draw(key_of[13], (D,), 0.3, 1.75, (), jnp.float32)
    cotangent = bell_draw_with(key_of[14], (TOKENS, D), 1.0, 6.0, ((0, 8),), (0, 1, 8, 2.0))
    return dict(tokens=tokens, segments=segments, first_gain=first_gain, first_shift=first_shift, second_gain=second_gain, second_shift=second_shift, inlet=inlet, offsets=offsets, outlet=outlet, outlet_bias=outlet_bias, expand=expand, thresholds=thresholds, contract=contract, contract_bias=contract_bias, cotangent=cotangent)


EPS = 1e-05

def layer_norm(value, gain, shift):
    center = value - lax.optimization_barrier(jnp.mean(value, axis=-1, keepdims=True))
    inverse = lax.rsqrt(lax.optimization_barrier(jnp.mean(center * center, axis=-1, keepdims=True)) + EPS)
    scaled = center * inverse
    return (scaled * gain + shift, scaled, inverse)

def norm_back(normed_grad, scaled, inverse, gain):
    lifted = normed_grad * gain
    return inverse * (lifted - lax.optimization_barrier(jnp.mean(lifted, axis=-1, keepdims=True)) - scaled * lax.optimization_barrier(jnp.mean(lifted * scaled, axis=-1, keepdims=True)))

def positions_of(labels):
    index = jnp.arange(labels.shape[0], dtype=jnp.int32)
    before = jnp.concatenate([jnp.full((1,), -2, jnp.int32), labels[:-1].astype(jnp.int32)])
    first = jnp.where(labels != before, index, jnp.zeros_like(index))
    return index - lax.cummax(first, axis=0)

def rotary_tables(labels):
    angles_pos = positions_of(labels).astype(jnp.float32)
    freq = jnp.exp(jnp.arange(ROT // 2, dtype=jnp.float32) * (-2.0 * math.log(10000.0) / ROT))
    angle = angles_pos[:, None] * freq[None, :]
    return (jnp.cos(angle)[:, None, :], jnp.sin(angle)[:, None, :])

def rotate(field, cosine, sine, direction):
    half = cosine.shape[-1]
    first = field[..., :half]
    second = field[..., half:2 * half]
    rest = field[..., 2 * half:]
    new_first = first * cosine - direction * second * sine
    new_second = second * cosine + direction * first * sine
    return jnp.concatenate([new_first, new_second, rest], axis=-1)

def gelu_pair(expanded):
    cumulative = 0.5 * (1.0 + lax.erf(expanded * (1.0 / math.sqrt(2.0))))
    density = jnp.exp(-0.5 * expanded * expanded) * (1.0 / math.sqrt(2.0 * math.pi))
    return (expanded * cumulative, cumulative + expanded * density)

def masked_scores(query_rows, keys, label_rows, label_keys, start):
    scores = jnp.einsum('qhd,khd->hqk', query_rows.astype(jnp.float32), keys.astype(jnp.float32)) * 0.125
    query_index = start + jnp.arange(query_rows.shape[0], dtype=jnp.int32)
    key_index = jnp.arange(keys.shape[0], dtype=jnp.int32)
    allowed = (label_rows[:, None] == label_keys[None, :]) & (key_index[None, :] <= query_index[:, None])
    return jnp.where(allowed[None], scores, -jnp.inf)

def layer_pass(tokens, cotangent, labels, first_gain, first_shift, second_gain, second_shift, inlet, offsets, outlet, outlet_bias, expand, thresholds, contract, contract_bias):
    count = tokens.shape[0]
    heads = offsets.shape[0]
    head_size = offsets.shape[1] // 3
    residual = tokens.astype(jnp.float32)
    normed_full, scaled_one, inverse_one = layer_norm(residual, first_gain, first_shift)
    normed_one = normed_full.astype(jnp.bfloat16)
    normed_full, scaled_two, inverse_two = layer_norm(residual, second_gain, second_shift)
    normed_two = normed_full.astype(jnp.bfloat16)
    projected = (jnp.dot(normed_one, inlet, preferred_element_type=jnp.float32) + offsets.reshape(-1)).reshape(count, heads, 3, head_size)
    cosine, sine = rotary_tables(labels)
    query = rotate(projected[:, :, 0], cosine, sine, 1.0).astype(jnp.bfloat16)
    key = rotate(projected[:, :, 1], cosine, sine, 1.0).astype(jnp.bfloat16)
    value = projected[:, :, 2].astype(jnp.bfloat16)
    width = min(512, count)
    pieces = []
    totals = []
    for start in range(0, count, width):
        end = start + width
        scores = masked_scores(query[start:end], key[:end], labels[start:end], labels[:end], start)
        peak = lax.optimization_barrier(jnp.max(scores, axis=-1, keepdims=True))
        log_total = peak + jnp.log(lax.optimization_barrier(jnp.sum(jnp.exp(scores - peak), axis=-1, keepdims=True)))
        softmax = jnp.exp(scores - log_total).astype(jnp.bfloat16)
        pieces.append(jnp.einsum('hqk,khd->qhd', softmax.astype(jnp.float32), value[:end].astype(jnp.float32)).astype(jnp.bfloat16))
        totals.append(log_total)
    attended = jnp.concatenate(pieces, axis=0).reshape(count, heads * head_size)
    expanded = jnp.dot(normed_two, expand, preferred_element_type=jnp.float32) + thresholds
    active_full, slope = gelu_pair(expanded)
    active = active_full.astype(jnp.bfloat16)
    branch = jnp.dot(attended, outlet, preferred_element_type=jnp.float32) + jnp.dot(active, contract, preferred_element_type=jnp.float32)
    mixed = (residual + branch + outlet_bias + contract_bias).astype(jnp.bfloat16)
    live = (labels >= 0).astype(jnp.float32)
    grad_full = cotangent.astype(jnp.float32) * live[:, None]
    grad_out = grad_full.astype(jnp.bfloat16)
    bias_grad = lax.optimization_barrier(jnp.sum(grad_full, axis=0))
    contract_grad = jnp.dot(active.T, grad_out, preferred_element_type=jnp.float32)
    outlet_grad = jnp.dot(attended.T, grad_out, preferred_element_type=jnp.float32)
    active_grad = jnp.dot(grad_out, contract.T, preferred_element_type=jnp.float32)
    expanded_grad = active_grad * slope
    expanded_back = expanded_grad.astype(jnp.bfloat16)
    expand_grad = jnp.dot(normed_two.T, expanded_back, preferred_element_type=jnp.float32)
    thresholds_grad = lax.optimization_barrier(jnp.sum(expanded_grad, axis=0))
    normed_two_grad = jnp.dot(expanded_back, expand.T, preferred_element_type=jnp.float32)
    attended_grad = jnp.dot(grad_out, outlet.T, preferred_element_type=jnp.float32).astype(jnp.bfloat16).reshape(count, heads, head_size)
    query_parts = []
    key_grad = jnp.zeros((count, heads, head_size), jnp.float32)
    value_grad = jnp.zeros((count, heads, head_size), jnp.float32)
    for number, start in enumerate(range(0, count, width)):
        end = start + width
        scores = masked_scores(query[start:end], key[:end], labels[start:end], labels[:end], start)
        weight_full = jnp.exp(scores - totals[number])
        softmax = weight_full.astype(jnp.bfloat16).astype(jnp.float32)
        rows_back = attended_grad[start:end].astype(jnp.float32)
        prob_grad = jnp.einsum('qhd,khd->hqk', rows_back, value[:end].astype(jnp.float32))
        delta = lax.optimization_barrier(jnp.sum(weight_full * prob_grad, axis=-1, keepdims=True))
        score_grad = (weight_full * (prob_grad - delta)).astype(jnp.bfloat16).astype(jnp.float32)
        query_parts.append(jnp.einsum('hqk,khd->qhd', score_grad, key[:end].astype(jnp.float32)) * 0.125)
        key_grad = key_grad.at[:end].add(jnp.einsum('hqk,qhd->khd', score_grad, query[start:end].astype(jnp.float32)) * 0.125)
        value_grad = value_grad.at[:end].add(jnp.einsum('hqk,qhd->khd', softmax, rows_back))
    query_grad = rotate(jnp.concatenate(query_parts, axis=0), cosine, sine, -1.0)
    key_grad = rotate(key_grad, cosine, sine, -1.0)
    inlet_full = jnp.stack([query_grad, key_grad, value_grad], axis=2).reshape(count, heads * 3 * head_size)
    inlet_back = inlet_full.astype(jnp.bfloat16)
    inlet_grad = jnp.dot(normed_one.T, inlet_back, preferred_element_type=jnp.float32)
    offsets_grad = lax.optimization_barrier(jnp.sum(inlet_full, axis=0)).reshape(heads, 3 * head_size)
    normed_one_grad = jnp.dot(inlet_back, inlet.T, preferred_element_type=jnp.float32)
    norm_grads = jnp.stack([lax.optimization_barrier(jnp.sum(normed_one_grad * scaled_one, axis=0)), lax.optimization_barrier(jnp.sum(normed_one_grad, axis=0)), lax.optimization_barrier(jnp.sum(normed_two_grad * scaled_two, axis=0)), lax.optimization_barrier(jnp.sum(normed_two_grad, axis=0))])
    local_grad = norm_back(normed_one_grad, scaled_one, inverse_one, first_gain) + norm_back(normed_two_grad, scaled_two, inverse_two, second_gain)
    input_grad = (grad_full + local_grad).astype(jnp.bfloat16)
    grads = (inlet_grad, offsets_grad, outlet_grad, expand_grad, thresholds_grad, contract_grad, bias_grad, norm_grads)
    return (mixed, input_grad, grads)

def reference(tokens, segments, first_gain, first_shift, second_gain, second_shift, inlet, offsets, outlet, outlet_bias, expand, thresholds, contract, contract_bias, cotangent):
    zeros = (jnp.zeros((D, H * 3 * HS), jnp.float32), jnp.zeros((H, 3 * HS), jnp.float32), jnp.zeros((H * HS, D), jnp.float32), jnp.zeros((D, FF), jnp.float32), jnp.zeros((FF,), jnp.float32), jnp.zeros((FF, D), jnp.float32), jnp.zeros((D,), jnp.float32), jnp.zeros((4, D), jnp.float32))

    def advance(carry, block):
        block_tokens, block_cot, block_labels = block
        mixed, input_grad, grads = layer_pass(block_tokens, block_cot, block_labels, first_gain, first_shift, second_gain, second_shift, inlet, offsets, outlet, outlet_bias, expand, thresholds, contract, contract_bias)
        return (tuple((total + extra for total, extra in zip(carry, grads))), (mixed, input_grad))
    carry, (mixed, input_grad) = lax.scan(advance, zeros, (tokens.reshape(N_DP, TOK_DEV, D), cotangent.reshape(N_DP, TOK_DEV, D), segments.reshape(N_DP, TOK_DEV)))
    inlet_grad, offsets_grad, outlet_grad, expand_grad, thresholds_grad, contract_grad, bias_grad, norm_grads = carry
    return (mixed.reshape(TOKENS, D), input_grad.reshape(TOKENS, D), inlet_grad, offsets_grad, outlet_grad, expand_grad, thresholds_grad.reshape(HU_GROUPS, GROUP_UNITS), contract_grad, bias_grad, norm_grads)
```

```python
import functools
import math

import jax
import jax.numpy as jnp
from jax import lax
from jax.experimental import pallas as pl
from jax.experimental.pallas import tpu as pltpu
from jax.sharding import PartitionSpec as P

ROT = 16
EPS = 1e-05
F32 = jnp.float32
BF16 = jnp.bfloat16
VMEM_LIMIT = 40 * 1024 * 1024


def dot(a, b):
    return jnp.dot(a, b, preferred_element_type=F32)


def dot_t(a, b):
    return lax.dot_general(a, b, (((1,), (1,)), ((), ())), preferred_element_type=F32)


def dot_rows(a, b):
    return lax.dot_general(a, b, (((0,), (0,)), ((), ())), preferred_element_type=F32)


def norm_parts(tok):
    x = tok.astype(F32)
    center = x - jnp.mean(x, axis=-1, keepdims=True)
    inverse = lax.rsqrt(jnp.mean(center * center, axis=-1, keepdims=True) + EPS)
    return center * inverse, inverse


def label_tables(seg_row):
    n = seg_row.shape[1]
    across = jnp.broadcast_to(seg_row, (n, n))
    down = across.T
    row = lax.broadcasted_iota(jnp.int32, (n, n), 0)
    col = lax.broadcasted_iota(jnp.int32, (n, n), 1)
    same = across == down
    allowed = same & (col <= row)
    position = jnp.sum(jnp.where(same & (row <= col), 1.0, 0.0), axis=0, keepdims=True) - 1.0
    live = jnp.where(down[:, :1] >= 0.0, 1.0, 0.0)
    return allowed, live, position


def rope_tables(position, heads, size, width):
    half = ROT // 2
    index = lax.broadcasted_iota(jnp.int32, (half, 1), 0).astype(F32)
    angle = jnp.exp(index * (-2.0 * math.log(10000.0) / ROT)) * position
    cosine = jnp.concatenate([jnp.cos(angle)] * (128 // half), axis=0).T
    sine = jnp.concatenate([jnp.sin(angle)] * (128 // half), axis=0).T
    lane = lax.broadcasted_iota(jnp.int32, (1, width), 1)
    part, dim = lane // size, lane % size
    value = part >= 3 * heads
    for head in range(heads):
        value = value | (part == 3 * head + 2)
    turned = jnp.logical_not(value) & (dim < ROT)
    low = turned & (dim < half)
    high = turned & (dim >= half)
    blocks = width // 128
    cosine = jnp.concatenate([cosine] * blocks, axis=1)
    sine = jnp.concatenate([sine] * blocks, axis=1)
    return (
        jnp.where(turned, cosine, 1.0),
        jnp.where(low, sine, 0.0),
        jnp.where(high, sine, 0.0),
    )


def turn(field, tables, sign):
    cosine, low, high = tables
    width = field.shape[1]
    ahead = pltpu.roll(field, width - ROT // 2, 1)
    behind = pltpu.roll(field, ROT // 2, 1)
    return field * cosine + sign * (behind * high - ahead * low)


def gelu_pair(expanded):
    cumulative = 0.5 * (1.0 + lax.erf(expanded * (1.0 / math.sqrt(2.0))))
    density = jnp.exp(-0.5 * expanded * expanded) * (1.0 / math.sqrt(2.0 * math.pi))
    return expanded * cumulative, cumulative + expanded * density


def ffn_block(normed_two, grad_out, expand, thresholds, contract):
    expanded = dot(normed_two, expand) + thresholds
    active, slope = gelu_pair(expanded)
    grad = dot_t(grad_out, contract) * slope
    return active.astype(BF16), grad


def attention_block(normed_one, grad_out, allowed, position, inlet_t, offsets, outlet, heads, size):
    n = normed_one.shape[0]
    columns = inlet_t.shape[0]
    width = -(-columns // 128) * 128
    tables = rope_tables(position, heads, size, width)
    projected = dot_t(normed_one, inlet_t) + offsets
    if width > columns:
        projected = jnp.concatenate([projected, jnp.zeros((n, width - columns), F32)], axis=1)
    turned = turn(projected, tables, 1.0).astype(BF16)
    attended_grad = dot_t(grad_out, outlet).astype(BF16)
    attended, grads = [], []
    for head in range(heads):
        at = 3 * head * size
        query = turned[:, at : at + size]
        key = turned[:, at + size : at + 2 * size]
        value = turned[:, at + 2 * size : at + 3 * size]
        back = attended_grad[:, head * size : (head + 1) * size]
        scores = jnp.where(allowed, dot_t(query, key) * 0.125, -jnp.inf)
        raised = jnp.exp(scores - jnp.max(scores, axis=-1, keepdims=True))
        weight = raised / jnp.sum(raised, axis=-1, keepdims=True)
        softmax = weight.astype(BF16)
        attended.append(dot(softmax, value).astype(BF16))
        prob_grad = dot_t(back, value)
        delta = jnp.sum(weight * prob_grad, axis=-1, keepdims=True)
        score_grad = (weight * (prob_grad - delta)).astype(BF16)
        grads.append(dot(score_grad, key) * 0.125)
        grads.append(dot_rows(score_grad, query) * 0.125)
        grads.append(dot_rows(softmax, back))
    if width > columns:
        grads.append(jnp.zeros((n, width - columns), F32))
    inlet_full = turn(jnp.concatenate(grads, axis=1), tables, -1.0)
    return jnp.concatenate(attended, axis=1), inlet_full


def own_kernel(
    heads, size,
    tok_ref, cot_ref, seg_ref, norm_ref, inlet_ref, offsets_ref, outlet_ref, expand_ref, thr_ref, contract_ref,
    sums_ref, active_ref, back_ref, attended_ref, inlet_back_ref, small_ref,
):
    allowed, live, position = label_tables(seg_ref[...])
    scaled, inverse = norm_parts(tok_ref[...])
    gain_one, shift_one = norm_ref[0:1], norm_ref[1:2]
    gain_two, shift_two = norm_ref[2:3], norm_ref[3:4]
    normed_one = (scaled * gain_one + shift_one).astype(BF16)
    normed_two = (scaled * gain_two + shift_two).astype(BF16)
    grad_full = cot_ref[...].astype(F32) * live
    grad_out = grad_full.astype(BF16)
    active, expanded_grad = ffn_block(
        normed_two, grad_out, expand_ref[...], thr_ref[...], contract_ref[...]
    )
    expanded_back = expanded_grad.astype(BF16)
    attended, inlet_full = attention_block(
        normed_one, grad_out, allowed, position, inlet_ref[...], offsets_ref[...], outlet_ref[...], heads, size
    )
    columns = inlet_ref.shape[0]
    inlet_back = inlet_full.astype(BF16)[:, :columns]
    active_ref[...] = active
    back_ref[...] = expanded_back
    attended_ref[...] = attended
    inlet_back_ref[...] = inlet_back
    branch = dot(attended, outlet_ref[...]) + dot(active, contract_ref[...])
    one_grad = dot(inlet_back, inlet_ref[...])
    two_grad = dot_t(expanded_back, expand_ref[...])
    lifted = one_grad * gain_one + two_grad * gain_two
    local = inverse * (
        lifted
        - jnp.mean(lifted, axis=-1, keepdims=True)
        - scaled * jnp.mean(lifted * scaled, axis=-1, keepdims=True)
    )
    sums_ref[0] = branch.astype(BF16)
    sums_ref[1] = local.astype(BF16)
    small_ref[...] = jnp.zeros_like(small_ref)
    small_ref[0:1] = jnp.sum(one_grad * scaled, axis=0, keepdims=True)
    small_ref[1:2] = jnp.sum(one_grad, axis=0, keepdims=True)
    small_ref[2:3] = jnp.sum(two_grad * scaled, axis=0, keepdims=True)
    small_ref[3:4] = jnp.sum(two_grad, axis=0, keepdims=True)
    small_ref[4:5] = jnp.sum(grad_full, axis=0, keepdims=True)
    small_ref[5:6, : thr_ref.shape[1]] = jnp.sum(expanded_grad, axis=0, keepdims=True)
    small_ref[6:7, :columns] = jnp.sum(inlet_full, axis=0, keepdims=True)[:, :columns]


def slabs(source, who_ref, send, dests, block):
    if dests == 1:
        return source[...]
    first = who_ref[1]
    first = 1 - first if send else first
    rows = []
    for rest in range(dests // 4):
        start = (4 * rest + 2 * who_ref[0] + first) * block
        rows.append(source[pl.ds(pl.multiple_of(start, 8), block), :])
    return jnp.concatenate(rows, axis=0) if len(rows) > 1 else rows[0]


def partner_inputs(who_ref, got_ref, swap_ref, n):
    core = who_ref[2]
    got, swap = got_ref[0:n], swap_ref[0:n]
    tok = jnp.where(core == 0, got, swap)
    cot = jnp.where(core == 0, swap, got)
    return tok, cot, got_ref[n : n + 1, :n].astype(F32)


def ffn_kernel(
    dests,
    who_ref, got_ref, swap_ref, tok_ref, cot_ref, seg_ref, norm_ref, expand_ref, thr_ref, contract_ref, active_ref, back_ref,
    send_ref, keep_ref,
    left_ref,
):
    n = tok_ref.shape[0]
    tok, cot, seg = partner_inputs(who_ref, got_ref, swap_ref, n)
    live = jnp.where(jnp.broadcast_to(seg, (128, n)).T[:, :1] >= 0.0, 1.0, 0.0)
    live_own = jnp.where(jnp.broadcast_to(seg_ref[...], (128, n)).T[:, :1] >= 0.0, 1.0, 0.0)
    gain, shift = norm_ref[2:3], norm_ref[3:4]
    scaled, _ = norm_parts(tok)
    normed = (scaled * gain + shift).astype(BF16)
    scaled, _ = norm_parts(tok_ref[...])
    normed_own = (scaled * gain + shift).astype(BF16)
    grad_out = (cot.astype(F32) * live).astype(BF16)
    grad_own = (cot_ref[...].astype(F32) * live_own).astype(BF16)
    active, grad = ffn_block(normed, grad_out, expand_ref[...], thr_ref[...], contract_ref[...])
    right = (
        jnp.concatenate([back_ref[...], grad.astype(BF16)], axis=0),
        jnp.concatenate([active_ref[...], active], axis=0),
    )
    left = (
        jnp.concatenate([normed_own, normed], axis=0),
        jnp.concatenate([grad_own, grad_out], axis=0),
    )
    block = left_ref.shape[0] // dests
    half = dests // 4 * block
    for which in range(2):
        left_ref[...] = left[which].T
        rows = jnp.concatenate(
            [slabs(left_ref, who_ref, True, dests, block), slabs(left_ref, who_ref, False, dests, block)], axis=0
        )
        product = dot(rows, right[which])
        send_ref[which] = product[:half].astype(BF16)
        keep_ref[which] = product[half:]


def attention_kernel(
    heads, size, dests,
    who_ref, got_ref, swap_ref, tok_ref, cot_ref, seg_ref, norm_ref, inlet_ref, offsets_ref, outlet_ref, attended_ref, inlet_back_ref,
    send_ref, keep_ref,
    left_ref,
):
    n = tok_ref.shape[0]
    tok, cot, seg = partner_inputs(who_ref, got_ref, swap_ref, n)
    allowed, live, position = label_tables(seg)
    live_own = jnp.where(jnp.broadcast_to(seg_ref[...], (128, n)).T[:, :1] >= 0.0, 1.0, 0.0)
    gain, shift = norm_ref[0:1], norm_ref[1:2]
    scaled, _ = norm_parts(tok)
    normed = (scaled * gain + shift).astype(BF16)
    scaled, _ = norm_parts(tok_ref[...])
    normed_own = (scaled * gain + shift).astype(BF16)
    grad_out = (cot.astype(F32) * live).astype(BF16)
    grad_own = (cot_ref[...].astype(F32) * live_own).astype(BF16)
    attended, inlet_full = attention_block(
        normed, grad_out, allowed, position, inlet_ref[...], offsets_ref[...], outlet_ref[...], heads, size
    )
    columns = inlet_ref.shape[0]
    inlet_back = inlet_full.astype(BF16)[:, :columns]
    block = left_ref.shape[0] // dests
    half = dests // 4 * block
    products = []
    for left, right in (
        ((normed_own, normed), (inlet_back_ref[...], inlet_back)),
        ((grad_own, grad_out), (attended_ref[...], attended)),
    ):
        left_ref[...] = jnp.concatenate(left, axis=0).T
        rows = jnp.concatenate(
            [slabs(left_ref, who_ref, True, dests, block), slabs(left_ref, who_ref, False, dests, block)], axis=0
        )
        products.append(dot(rows, jnp.concatenate(right, axis=0)))
    product = jnp.concatenate(products, axis=1)
    send_ref[...] = product[:half].astype(BF16)
    keep_ref[...] = product[half:]


def call(kernel, outs, args, scratch=(), scalars=0):
    specs = [pl.BlockSpec(memory_space=pltpu.SMEM)] * scalars
    specs += [pl.BlockSpec(memory_space=pltpu.VMEM)] * (len(args) - scalars)
    return pl.pallas_call(
        kernel,
        out_shape=[jax.ShapeDtypeStruct(shape, dtype) for shape, dtype in outs],
        in_specs=specs,
        out_specs=[pl.BlockSpec(memory_space=pltpu.VMEM)] * len(outs),
        scratch_shapes=list(scratch),
        compiler_params=pltpu.CompilerParams(vmem_limit_bytes=VMEM_LIMIT),
    )(*args)


def swap(value, axis, count, bit):
    return lax.ppermute(value, axis, [(i, i ^ bit) for i in range(count)])


def finish(keep, got, me, n_dp):
    total = keep + got.astype(F32)
    bit = 4
    while bit < n_dp:
        lead = total.shape[:-3]
        split = total.reshape(lead + (-1, 2) + total.shape[-2:])
        low, high = split[..., 0, :, :], split[..., 1, :, :]
        up = (me & bit) != 0
        away = jnp.where(up, low, high).astype(BF16)
        total = jnp.where(up, high, low) + swap(away, "dp", n_dp, bit).astype(F32)
        bit *= 2
    return jnp.squeeze(total, axis=-3)


def body(n_dp, n_tensor, tokens, segments, first_gain, first_shift, second_gain, second_shift, inlet, offsets,
         outlet, outlet_bias, expand, thresholds, contract, contract_bias, cotangent):
    n, width = tokens.shape
    heads, size = offsets.shape[0], offsets.shape[1] // 3
    units = expand.shape[1]
    columns = inlet.shape[1]
    mine = outlet.shape[0]
    block = width // n_dp
    dests = n_dp
    me = lax.axis_index("dp")
    you = lax.axis_index("tensor")
    core = you & 1
    who = jnp.stack([(me >> 1) & 1, me & 1, core, you]).astype(jnp.int32)
    seg_row = segments.astype(F32)[None, :]
    norms = jnp.stack([first_gain, first_shift, second_gain, second_shift])
    inlet_t = inlet.T
    offsets_row = offsets.reshape(1, columns)
    thr_row = thresholds[None, :]

    labels = jnp.broadcast_to(
        jnp.pad(seg_row.astype(BF16), ((0, 0), (0, width - n))), (16, width)
    )
    payload = jnp.concatenate([jnp.where(core == 0, tokens, cotangent), labels], axis=0)
    got = swap(payload, "dp", n_dp, 2)
    other = swap(got, "tensor", n_tensor, 1)

    sums, active, back, attended, inlet_back, small = call(
        functools.partial(own_kernel, heads, size),
        [((2, n, width), BF16), ((n, units), BF16), ((n, units), BF16), ((n, mine), BF16), ((n, columns), BF16), ((8, width), F32)],
        [tokens, cotangent, seg_row, norms, inlet_t, offsets_row, outlet, expand, thr_row, contract],
    )
    half = dests // 4 * block
    ffn_send, ffn_keep = call(
        functools.partial(ffn_kernel, dests),
        [((2, half, units), BF16), ((2, half, units), F32)],
        [who, got, other, tokens, cotangent, seg_row, norms, expand, thr_row, contract, active, back],
        [pltpu.VMEM((width, 2 * n), BF16)],
        1,
    )
    att_send, att_keep = call(
        functools.partial(attention_kernel, heads, size, dests),
        [((half, columns + mine), BF16), ((half, columns + mine), F32)],
        [who, got, other, tokens, cotangent, seg_row, norms, inlet_t, offsets_row, outlet, attended, inlet_back],
        [pltpu.VMEM((width, 2 * n), BF16)],
        1,
    )
    ffn_got = swap(ffn_send, "dp", n_dp, 1)
    att_got = swap(att_send, "dp", n_dp, 1)
    ffn = finish(
        ffn_keep.reshape(2, -1, block, units), ffn_got.reshape(2, -1, block, units), me, n_dp
    )
    att = finish(
        att_keep.reshape(-1, block, columns + mine), att_got.reshape(-1, block, columns + mine), me, n_dp
    )

    first = jnp.where(core == 0, sums[0], sums[1]).astype(F32)
    part = first + swap(jnp.where(core == 0, sums[1], sums[0]), "tensor", n_tensor, 1).astype(F32)
    bit = 2
    while bit < n_tensor:
        part = part.astype(BF16)
        part = part.astype(F32) + swap(part, "tensor", n_tensor, bit).astype(F32)
        bit *= 2
    live = (segments >= 0).astype(F32)[:, None]
    base = jnp.where(
        core == 0,
        tokens.astype(F32) + (outlet_bias + contract_bias),
        cotangent.astype(F32) * live,
    )
    done = (base + part).astype(BF16)
    paired = swap(done, "tensor", n_tensor, 1)
    mixed = jnp.where(core == 0, done, paired)
    input_grad = jnp.where(core == 0, paired, done)

    by_dest = small[:6].reshape(6, n_dp, block).transpose(1, 0, 2)
    third = offsets.shape[1] // n_dp
    offs = small[6, :columns].reshape(heads, n_dp, third).transpose(1, 0, 2)
    offs = jnp.pad(offs, ((0, 0), (0, 8 - heads), (0, block - third)))
    tile = jnp.concatenate([by_dest, jnp.zeros((n_dp, 2, block), F32), offs], axis=1)
    here = (jnp.arange(n_tensor) == you)[None, :, None, None]
    everywhere = (jnp.arange(16) < 4)[None, None, :, None]
    tile = jnp.where(here | everywhere, tile[:, None], 0.0)
    tile = lax.all_to_all(tile.reshape(n_dp * n_tensor, 16, block), ("dp", "tensor"), 0, 0, tiled=True)
    tile = jnp.sum(tile, axis=0)
    return (
        mixed,
        input_grad,
        att[:, :columns],
        tile[8 : 8 + heads, :third],
        att[:, columns:].T,
        ffn[0],
        tile[5:6],
        ffn[1].T,
        tile[4],
        tile[0:4],
    )


def solution(mesh):
    placed = (
        P("dp", None), P("dp"), P(), P(), P(), P(), P(None, "tensor"), P("tensor", None), P("tensor", None),
        P(), P(None, "tensor"), P("tensor"), P("tensor", None), P(), P("dp", None),
    )
    return jax.shard_map(
        functools.partial(body, mesh.shape["dp"], mesh.shape["tensor"]),
        mesh=mesh,
        in_specs=placed,
        out_specs=(
            P("dp", None), P("dp", None), P("dp", "tensor"), P("tensor", "dp"), P("tensor", "dp"),
            P("dp", "tensor"), P("tensor", "dp"), P("tensor", "dp"), P("dp"), P(None, "dp"),
        ),
        check_vma=False,
    )
```

```python
import functools
import math

import jax
import jax.numpy as jnp
from jax import lax
from jax.experimental import pallas as pl
from jax.experimental.pallas import tpu as pltpu
from jax.sharding import PartitionSpec as P


ROT = 16
EPS = 1e-05
F32 = jnp.float32
BF16 = jnp.bfloat16
MIB = 1024 * 1024
VMEM_LIMIT = 32 * MIB


def dot(a, b):
    return jnp.dot(a, b, preferred_element_type=F32)


def dot_t(a, b):
    return lax.dot_general(a, b, (((1,), (1,)), ((), ())), preferred_element_type=F32)


def dot_rows(a, b):
    return lax.dot_general(a, b, (((0,), (0,)), ((), ())), preferred_element_type=F32)


def norm_parts(tok):
    x = tok.astype(F32)
    center = x - jnp.mean(x, axis=-1, keepdims=True)
    inverse = lax.rsqrt(jnp.mean(center * center, axis=-1, keepdims=True) + EPS)
    return center * inverse, inverse


def label_tables(seg_row):
    n = seg_row.shape[1]
    across = jnp.broadcast_to(seg_row, (n, n))
    down = across.T
    row = lax.broadcasted_iota(jnp.int32, (n, n), 0)
    col = lax.broadcasted_iota(jnp.int32, (n, n), 1)
    same = across == down
    allowed = same & (col <= row)
    position = jnp.sum(jnp.where(same & (row <= col), 1.0, 0.0), axis=0, keepdims=True) - 1.0
    live = jnp.where(down[:, :1] >= 0.0, 1.0, 0.0)
    return allowed, live, position


def rope_tables(position, heads, size, width):
    half = ROT // 2
    index = lax.broadcasted_iota(jnp.int32, (half, 1), 0).astype(F32)
    angle = jnp.exp(index * (-2.0 * math.log(10000.0) / ROT)) * position
    cosine = jnp.concatenate([jnp.cos(angle)] * (128 // half), axis=0).T
    sine = jnp.concatenate([jnp.sin(angle)] * (128 // half), axis=0).T
    lane = lax.broadcasted_iota(jnp.int32, (1, width), 1)
    part, dim = lane // size, lane % size
    value = part >= 3 * heads
    for head in range(heads):
        value = value | (part == 3 * head + 2)
    turned = jnp.logical_not(value) & (dim < ROT)
    low = turned & (dim < half)
    high = turned & (dim >= half)
    blocks = width // 128
    cosine = jnp.concatenate([cosine] * blocks, axis=1)
    sine = jnp.concatenate([sine] * blocks, axis=1)
    return (
        jnp.where(turned, cosine, 1.0),
        jnp.where(low, sine, 0.0),
        jnp.where(high, sine, 0.0),
    )


def turn(field, tables, sign):
    cosine, low, high = tables
    width = field.shape[1]
    ahead = pltpu.roll(field, width - ROT // 2, 1)
    behind = pltpu.roll(field, ROT // 2, 1)
    return field * cosine + sign * (behind * high - ahead * low)


def gelu_pair(expanded):
    cumulative = 0.5 * (1.0 + lax.erf(expanded * (1.0 / math.sqrt(2.0))))
    density = jnp.exp(-0.5 * expanded * expanded) * (1.0 / math.sqrt(2.0 * math.pi))
    return expanded * cumulative, cumulative + expanded * density


def ffn_block(normed_two, grad_out, expand, thresholds, contract):
    expanded = dot(normed_two, expand) + thresholds
    active, slope = gelu_pair(expanded)
    grad = dot_t(grad_out, contract) * slope
    return active.astype(BF16), grad


def attention_block(normed_one, grad_out, allowed, position, inlet_t, offsets, outlet, heads, size):
    n = normed_one.shape[0]
    columns = inlet_t.shape[0]
    width = -(-columns // 128) * 128
    tables = rope_tables(position, heads, size, width)
    projected = dot_t(normed_one, inlet_t) + offsets
    if width > columns:
        projected = jnp.concatenate([projected, jnp.zeros((n, width - columns), F32)], axis=1)
    turned = turn(projected, tables, 1.0).astype(BF16)
    attended_grad = dot_t(grad_out, outlet).astype(BF16)
    attended, grads = [], []
    for head in range(heads):
        at = 3 * head * size
        query = turned[:, at : at + size]
        key = turned[:, at + size : at + 2 * size]
        value = turned[:, at + 2 * size : at + 3 * size]
        back = attended_grad[:, head * size : (head + 1) * size]
        scores = jnp.where(allowed, dot_t(query, key) * 0.125, -jnp.inf)
        raised = jnp.exp(scores - jnp.max(scores, axis=-1, keepdims=True))
        weight = raised / jnp.sum(raised, axis=-1, keepdims=True)
        softmax = weight.astype(BF16)
        attended.append(dot(softmax, value).astype(BF16))
        prob_grad = dot_t(back, value)
        delta = jnp.sum(weight * prob_grad, axis=-1, keepdims=True)
        score_grad = (weight * (prob_grad - delta)).astype(BF16)
        grads.append(dot(score_grad, key) * 0.125)
        grads.append(dot_rows(score_grad, query) * 0.125)
        grads.append(dot_rows(softmax, back))
    if width > columns:
        grads.append(jnp.zeros((n, width - columns), F32))
    inlet_full = turn(jnp.concatenate(grads, axis=1), tables, -1.0)
    return jnp.concatenate(attended, axis=1), inlet_full


def flat(ref):
    rows = [ref[i : i + 1, :] for i in range(ref.shape[0])]
    return jnp.concatenate(rows, axis=1) if len(rows) > 1 else rows[0]


def folded(value):
    size = value.shape[0]
    return value.reshape(size // 128, 128) if size % 128 == 0 else value.reshape(1, size)


def label_row(seg_ref):
    return flat(seg_ref).astype(F32)


def live_column(seg_row):
    down = jnp.broadcast_to(seg_row, (128, seg_row.shape[1])).T
    return jnp.where(down[:, :1] >= 0.0, 1.0, 0.0)


def gather_kernel(tok_ref, cot_ref, seg_ref, out_ref, sem):
    n = tok_ref.shape[0]

    @pl.when(core_bit() == 0)
    def _():
        pltpu.make_async_copy(tok_ref, out_ref.at[0:n], sem).start()

    @pl.when(core_bit() != 0)
    def _():
        pltpu.make_async_copy(cot_ref, out_ref.at[0:n], sem).start()

    width = out_ref.shape[1]
    row = label_row(seg_ref)
    row = jnp.concatenate([row, jnp.zeros((1, width - n), F32)], axis=1)
    out_ref[n : n + 16] = jnp.broadcast_to(row, (16, width)).astype(BF16)
    pltpu.make_async_copy(tok_ref, out_ref.at[0:n], sem).wait()


def own_kernel(
    heads, size, n_dp, n_tensor,
    tok_any, cot_any, seg_ref, gain_one_ref, shift_one_ref, gain_two_ref, shift_two_ref, offsets_ref, thr_ref,
    inlet_any, outlet_any, expand_any, contract_any,
    tok_ref, cot_ref, inlet_ref, outlet_ref, expand_ref, contract_ref,
    away_ref, keep_ref, active_ref, back_ref, attended_ref, inlet_back_ref, tile_ref,
    sems,
):
    copies = [
        pltpu.make_async_copy(a, b, sems.at[i])
        for i, (a, b) in enumerate(
            [(tok_any, tok_ref), (cot_any, cot_ref), (expand_any, expand_ref), (contract_any, contract_ref),
             (inlet_any, inlet_ref), (outlet_any, outlet_ref)]
        )
    ]
    for copy in copies:
        copy.start()
    seg_row = label_row(seg_ref)
    allowed, live, position = label_tables(seg_row)
    gain_one, shift_one = flat(gain_one_ref), flat(shift_one_ref)
    gain_two, shift_two = flat(gain_two_ref), flat(shift_two_ref)
    offsets = jnp.concatenate([offsets_ref[i : i + 1, :] for i in range(heads)], axis=1)
    thr = flat(thr_ref)
    copies[0].wait()
    scaled, inverse = norm_parts(tok_ref[...])
    normed_one = (scaled * gain_one + shift_one).astype(BF16)
    normed_two = (scaled * gain_two + shift_two).astype(BF16)
    copies[1].wait()
    grad_full = cot_ref[...].astype(F32) * live
    grad_out = grad_full.astype(BF16)
    copies[2].wait()
    copies[3].wait()
    active, expanded_grad = ffn_block(normed_two, grad_out, expand_ref[...], thr, contract_ref[...])
    expanded_back = expanded_grad.astype(BF16)
    copies[4].wait()
    copies[5].wait()
    attended, inlet_full = attention_block(
        normed_one, grad_out, allowed, position, inlet_ref[...], offsets, outlet_ref[...], heads, size
    )
    columns = inlet_ref.shape[0]
    inlet_back = inlet_full.astype(BF16)[:, :columns]
    active_ref[...] = active
    back_ref[...] = expanded_back
    attended_ref[...] = attended
    inlet_back_ref[...] = inlet_back
    branch = dot(attended, outlet_ref[...]) + dot(active, contract_ref[...])
    one_grad = dot(inlet_back, inlet_ref[...])
    two_grad = dot_t(expanded_back, expand_ref[...])
    lifted = one_grad * gain_one + two_grad * gain_two
    local = inverse * (
        lifted
        - jnp.mean(lifted, axis=-1, keepdims=True)
        - scaled * jnp.mean(lifted * scaled, axis=-1, keepdims=True)
    )
    core = core_bit()
    away_ref[...] = jnp.where(core == 0, local, branch).astype(BF16)
    keep_ref[...] = jnp.where(core == 0, branch, local)

    def total(field):
        return jnp.sum(field, axis=0, keepdims=True)

    everyone = jnp.concatenate(
        [total(one_grad * scaled), total(one_grad), total(two_grad * scaled), total(two_grad)], axis=0
    )
    bias = total(grad_full)
    hidden = total(expanded_grad)
    shares = total(inlet_full)
    block = tile_ref.shape[3]
    third = 3 * size // n_dp
    per_dp = hidden.shape[1] // n_dp
    tile_ref[...] = jnp.zeros_like(tile_ref)
    for d in range(n_dp):
        lanes = slice(d * block, (d + 1) * block)
        for t in range(n_tensor):
            tile_ref[d, t, 0:4] = everyone[:, lanes]

        def put(t, d=d, lanes=lanes):
            tile_ref[d, t, 4:5] = bias[:, lanes]
            tile_ref[d, t, 5:6, :per_dp] = hidden[:, d * per_dp : (d + 1) * per_dp]
            for head in range(heads):
                at = head * 3 * size + d * third
                tile_ref[d, t, 8 + head : 9 + head, :third] = shares[:, at : at + third]

        put(lax.axis_index("tensor"))


def gather_bit():
    return lax.axis_index("dp") // 2 % 2


def first_bit():
    return lax.axis_index("dp") % 2


def core_bit():
    return lax.axis_index("tensor") % 2


def spread_rows(left, left_ref, dests):
    width = left.shape[1]
    block = width // dests
    if block % 16 == 0:
        left_ref[...] = left.T
        rows = []
        for flip in (1, 0):
            first = first_bit() if flip == 0 else 1 - first_bit()
            for rest in range(dests // 4):
                start = (4 * rest + 2 * gather_bit() + first) * block
                rows.append(left_ref[pl.ds(pl.multiple_of(start, 16), block), :])
        return jnp.concatenate(rows, axis=0)
    half = dests // 4 * block
    row = lax.broadcasted_iota(jnp.int32, (2 * half, width), 0)
    col = lax.broadcasted_iota(jnp.int32, (2 * half, width), 1)
    kept = row >= half
    row = jnp.where(kept, row - half, row)
    first = jnp.where(kept, first_bit(), 1 - first_bit())
    want = row + (row // block) * 3 * block + (2 * gather_bit() + first) * block
    return dot_t(jnp.where(want == col, 1.0, 0.0).astype(BF16), left).astype(BF16)


def partner_inputs(got_ref, swap_ref, n):
    core = core_bit()
    got, swapped = got_ref[0:n], swap_ref[0:n]
    tok = jnp.where(core == 0, got, swapped)
    cot = jnp.where(core == 0, swapped, got)
    return tok, cot, got_ref[n : n + 1, :n].astype(F32)


def put_halves(product, send_ref, keep_ref):
    half = product.shape[0] // 2
    send_ref[...] = product[:half].astype(BF16)
    keep_ref[...] = product[half:]


def expand_kernel(
    dests,
    got_ref, swap_ref, tok_ref, gain_ref, shift_ref, expand_ref, thr_ref, contract_ref, back_ref,
    send_ref, keep_ref, active_ref,
    left_ref,
):
    n = tok_ref.shape[0]
    tok, cot, seg = partner_inputs(got_ref, swap_ref, n)
    gain, shift = flat(gain_ref), flat(shift_ref)
    scaled, _ = norm_parts(tok)
    normed = (scaled * gain + shift).astype(BF16)
    scaled, _ = norm_parts(tok_ref[...])
    normed_own = (scaled * gain + shift).astype(BF16)
    grad_out = (cot.astype(F32) * live_column(seg)).astype(BF16)
    active, grad = ffn_block(normed, grad_out, expand_ref[...], flat(thr_ref), contract_ref[...])
    active_ref[...] = active
    rows = spread_rows(jnp.concatenate([normed_own, normed], axis=0), left_ref, dests)
    put_halves(dot(rows, jnp.concatenate([back_ref[...], grad.astype(BF16)], axis=0)), send_ref, keep_ref)


def contract_kernel(
    dests,
    got_ref, swap_ref, cot_ref, seg_ref, own_ref, active_ref,
    send_ref, keep_ref,
    left_ref,
):
    n = cot_ref.shape[0]
    _, cot, seg = partner_inputs(got_ref, swap_ref, n)
    grad_out = (cot.astype(F32) * live_column(seg)).astype(BF16)
    grad_own = (cot_ref[...].astype(F32) * live_column(label_row(seg_ref))).astype(BF16)
    rows = spread_rows(jnp.concatenate([grad_own, grad_out], axis=0), left_ref, dests)
    put_halves(dot(rows, jnp.concatenate([own_ref[...], active_ref[...]], axis=0)), send_ref, keep_ref)


def attention_kernel(
    heads, size, dests,
    got_ref, swap_ref, tok_ref, cot_ref, seg_ref, gain_ref, shift_ref, inlet_ref, offsets_ref, outlet_ref, attended_ref, inlet_back_ref, after_ref,
    send_ref, keep_ref,
    left_ref,
):
    n = tok_ref.shape[0]
    tok, cot, seg = partner_inputs(got_ref, swap_ref, n)
    allowed, live, position = label_tables(seg)
    gain, shift = flat(gain_ref), flat(shift_ref)
    offsets = jnp.concatenate([offsets_ref[i : i + 1, :] for i in range(heads)], axis=1)
    scaled, _ = norm_parts(tok)
    normed = (scaled * gain + shift).astype(BF16)
    scaled, _ = norm_parts(tok_ref[...])
    normed_own = (scaled * gain + shift).astype(BF16)
    grad_out = (cot.astype(F32) * live).astype(BF16)
    grad_own = (cot_ref[...].astype(F32) * live_column(label_row(seg_ref))).astype(BF16)
    attended, inlet_full = attention_block(
        normed, grad_out, allowed, position, inlet_ref[...], offsets, outlet_ref[...], heads, size
    )
    columns = inlet_ref.shape[0]
    inlet_back = inlet_full.astype(BF16)[:, :columns]
    rows = spread_rows(jnp.concatenate([normed_own, normed], axis=0), left_ref, dests)
    first = dot(rows, jnp.concatenate([inlet_back_ref[...], inlet_back], axis=0))
    rows = spread_rows(jnp.concatenate([grad_own, grad_out], axis=0), left_ref, dests)
    second = dot(rows, jnp.concatenate([attended_ref[...], attended], axis=0))
    put_halves(jnp.concatenate([first, second], axis=1), send_ref, keep_ref)


def halve_kernel(step, keep_ref, got_ref, send_ref, left_ref):
    bit = jnp.where((lax.axis_index("dp") & step) != 0, 1, 0)
    for i in range(send_ref.shape[0]):
        away, stay = 2 * i + 1 - bit, 2 * i + bit
        send_ref[i] = (keep_ref[away] + got_ref[away].astype(F32)).astype(BF16)
        left_ref[i] = keep_ref[stay] + got_ref[stay].astype(F32)


def add_kernel(keep_ref, got_ref, out_ref):
    out_ref[...] = keep_ref[0] + got_ref[0].astype(F32)


def split_kernel(keep_ref, got_ref, inlet_ref, outlet_ref):
    total = keep_ref[0] + got_ref[0].astype(F32)
    columns = inlet_ref.shape[1]
    inlet_ref[...] = total[:, :columns]
    outlet_ref[...] = total[:, columns:].T


def part_kernel(keep_ref, got_ref, out_ref):
    out_ref[...] = (keep_ref[...].astype(F32) + got_ref[...].astype(F32)).astype(BF16)


def done_kernel(part_ref, got_ref, tok_ref, cot_ref, seg_ref, bias_ref, other_ref, out_ref):
    part = part_ref[...].astype(F32) + got_ref[...].astype(F32)
    shift = flat(bias_ref) + flat(other_ref)
    live = live_column(label_row(seg_ref))
    base = jnp.where(core_bit() == 0, tok_ref[...].astype(F32) + shift, cot_ref[...].astype(F32) * live)
    out_ref[...] = (base + part).astype(BF16)


def pair_kernel(own_ref, got_ref, mixed_ref, grad_ref):
    first = core_bit() == 0
    own, got = own_ref[...], got_ref[...]
    mixed_ref[...] = jnp.where(first, own, got)
    grad_ref[...] = jnp.where(first, got, own)


def small_kernel(heads, third, tile_ref, norms_ref, bias_ref, thr_ref, offsets_ref):
    total = tile_ref[0]
    for i in range(1, tile_ref.shape[0]):
        total = total + tile_ref[i]
    norms_ref[...] = total[0:4]
    bias_ref[...] = total[4:5]
    thr_ref[...] = total[5:6, : thr_ref.shape[1]]
    offsets_ref[...] = total[8 : 8 + heads, :third]


def call(kernel, outs, args, flops=0, scratch=(), limit=VMEM_LIMIT, places="", results=""):
    kinds = {"v": pl.BlockSpec(memory_space=pltpu.VMEM), "a": pl.BlockSpec(memory_space=pltpu.HBM), "d": pl.BlockSpec()}
    places = places or "v" * len(args)
    results = results or "v" * len(outs)
    moved = sum(math.prod(s) * jnp.dtype(t).itemsize for s, t in outs)
    moved += sum(math.prod(a.shape) * a.dtype.itemsize for a in args)
    args = [pltpu.with_memory_space_constraint(a, pltpu.HBM) if k == "a" else a for a, k in zip(args, places)]
    return pl.pallas_call(
        kernel,
        out_shape=[jax.ShapeDtypeStruct(shape, dtype) for shape, dtype in outs],
        in_specs=[kinds[k] for k in places],
        out_specs=[kinds[k] for k in results],
        scratch_shapes=list(scratch),
        compiler_params=pltpu.CompilerParams(vmem_limit_bytes=limit),
        cost_estimate=pl.CostEstimate(flops=int(flops), bytes_accessed=moved, transcendentals=0),
    )(*args)


def swap(value, axis, count, bit):
    return lax.ppermute(value, axis, [(i, i ^ bit) for i in range(count)])


def step(n_dp, n_tensor, tokens, segments, first_gain, first_shift, second_gain, second_shift, inlet, offsets,
         outlet, outlet_bias, expand, thresholds, contract, contract_bias, cotangent):
    n, width = tokens.shape
    heads, size = offsets.shape[0], offsets.shape[1] // 3
    units = expand.shape[1]
    columns = inlet.shape[1]
    mine = outlet.shape[0]
    block = width // n_dp
    seg = folded(segments)
    gain_one, shift_one, gain_two, shift_two = map(folded, (first_gain, first_shift, second_gain, second_shift))
    thr = folded(thresholds)

    payload, = call(
        gather_kernel, [((n + 16, width), BF16)], [tokens, cotangent, seg],
        scratch=[pltpu.SemaphoreType.DMA], places="aav",
    )
    got = swap(payload, "dp", n_dp, 2)
    other = swap(got, "tensor", n_tensor, 1)

    (tok, cot, inlet_v, outlet_v, expand_v, contract_v, away, keep, active, back, attended, inlet_back, tile) = call(
        functools.partial(own_kernel, heads, size, n_dp, n_tensor),
        [(tokens.shape, BF16), (cotangent.shape, BF16), ((columns, width), BF16), (outlet.shape, BF16), (expand.shape, BF16),
         (contract.shape, BF16), ((n, width), BF16), ((n, width), F32), ((n, units), BF16), ((n, units), BF16),
         ((n, mine), BF16), ((n, columns), BF16), ((n_dp, n_tensor, 16, block), F32)],
        [tokens, cotangent, seg, gain_one, shift_one, gain_two, shift_two, offsets, thr, inlet.T, outlet, expand, contract],
        flops=6e9, scratch=[pltpu.SemaphoreType.DMA((6,))], places="aavvvvvvvaaaa",
    )
    half = n_dp // 4 * block
    left = [pltpu.VMEM((width, 2 * n), BF16)]

    expand_send, expand_keep, active_near = call(
        functools.partial(expand_kernel, n_dp),
        [((half, units), BF16), ((half, units), F32), ((n, units), BF16)],
        [got, other, tok, gain_two, shift_two, expand_v, thr, contract_v, back],
        flops=3e9, scratch=left,
    )
    expand_got = swap(expand_send, "dp", n_dp, 1)
    contract_send, contract_keep = call(
        functools.partial(contract_kernel, n_dp),
        [((half, units), BF16), ((half, units), F32)],
        [got, other, cot, seg, active, active_near],
        flops=1e9, scratch=left,
    )
    contract_got = swap(contract_send, "dp", n_dp, 1)
    tail_send, tail_keep = call(
        functools.partial(attention_kernel, heads, size, n_dp),
        [((half, columns + mine), BF16), ((half, columns + mine), F32)],
        [got, other, tok, cot, seg, gain_one, shift_one, inlet_v, offsets, outlet_v, attended, inlet_back, contract_keep],
        flops=5e9, scratch=left,
    )
    tail_got = swap(tail_send, "dp", n_dp, 1)

    part = keep
    near = swap(away, "tensor", n_tensor, 1)
    part, = call(part_kernel, [((n, width), BF16)], [keep, near], flops=1e6)
    bit = 2
    while 2 * bit < n_tensor:
        part, = call(part_kernel, [((n, width), BF16)], [part, swap(part, "tensor", n_tensor, bit)])
        bit *= 2
    far = swap(part, "tensor", n_tensor, bit)
    done, = call(
        done_kernel, [((n, width), BF16)],
        [part, far, tok, cot, seg, folded(outlet_bias), folded(contract_bias)], flops=1e6,
    )
    paired = swap(done, "tensor", n_tensor, 1)
    mixed, input_grad = call(pair_kernel, [((n, width), BF16)] * 2, [done, paired], results="dd")

    tile = lax.all_to_all(tile.reshape(n_dp * n_tensor, 16, block), ("dp", "tensor"), 0, 0, tiled=True)
    third = offsets.shape[1] // n_dp
    norm_grads, bias_grad, thr_grad, offsets_grad = call(
        functools.partial(small_kernel, heads, third),
        [((4, block), F32), ((1, block), F32), ((1, units // n_dp), F32), ((heads, third), F32)], [tile], results="dddd",
    )

    def reduce(kept, arrived):
        columns_here = kept.shape[1]
        kept = kept.reshape(-1, block, columns_here)
        arrived = arrived.reshape(-1, block, columns_here)
        bit = 4
        while bit < n_dp:
            rest = kept.shape[0] // 2
            shape = (rest, block, columns_here)
            away, kept = call(
                functools.partial(halve_kernel, bit), [(shape, BF16), (shape, F32)], [kept, arrived],
                flops=1e6,
            )
            arrived = swap(away, "dp", n_dp, bit)
            bit *= 2
        return kept, arrived

    expand_grad, = call(add_kernel, [((block, units), F32)], reduce(expand_keep, expand_got), results="d")
    contract_grad, = call(add_kernel, [((block, units), F32)], reduce(contract_keep, contract_got), results="d")
    inlet_grad, outlet_grad = call(
        split_kernel, [((block, columns), F32), ((mine, block), F32)],
        reduce(tail_keep, tail_got), results="dd",
    )
    return (
        mixed, input_grad, inlet_grad, offsets_grad, outlet_grad, expand_grad, thr_grad, contract_grad.T,
        bias_grad.reshape(block), norm_grads,
    )


def solution(mesh):
    placed = (
        P("dp", None), P("dp"), P(), P(), P(), P(), P(None, "tensor"), P("tensor", None), P("tensor", None),
        P(), P(None, "tensor"), P("tensor"), P("tensor", None), P(), P("dp", None),
    )
    return jax.shard_map(
        functools.partial(step, mesh.shape["dp"], mesh.shape["tensor"]),
        mesh=mesh,
        in_specs=placed,
        out_specs=(
            P("dp", None), P("dp", None), P("dp", "tensor"), P("tensor", "dp"), P("tensor", "dp"),
            P("dp", "tensor"), P("tensor", "dp"), P("tensor", "dp"), P("dp"), P(None, "dp"),
        ),
        check_vma=False,
    )
```

```python
import functools
import math

import jax
import jax.numpy as jnp
from jax import lax
from jax.experimental import pallas as pl
from jax.experimental.pallas import tpu as pltpu
from jax.sharding import PartitionSpec as P


ROT = 16
EPS = 1e-05
F32 = jnp.float32
BF16 = jnp.bfloat16
MIB = 1024 * 1024
VMEM_LIMIT = 32 * MIB


def dot(a, b):
    return jnp.dot(a, b, preferred_element_type=F32)


def dot_t(a, b):
    return lax.dot_general(a, b, (((1,), (1,)), ((), ())), preferred_element_type=F32)


def dot_rows(a, b):
    return lax.dot_general(a, b, (((0,), (0,)), ((), ())), preferred_element_type=F32)


def norm_parts(tok):
    x = tok.astype(F32)
    center = x - jnp.mean(x, axis=-1, keepdims=True)
    inverse = lax.rsqrt(jnp.mean(center * center, axis=-1, keepdims=True) + EPS)
    return center * inverse, inverse


def label_tables(seg_row):
    n = seg_row.shape[1]
    across = jnp.broadcast_to(seg_row, (n, n))
    down = across.T
    row = lax.broadcasted_iota(jnp.int32, (n, n), 0)
    col = lax.broadcasted_iota(jnp.int32, (n, n), 1)
    same = across == down
    allowed = same & (col <= row)
    position = jnp.sum(jnp.where(same & (row <= col), 1.0, 0.0), axis=0, keepdims=True) - 1.0
    live = jnp.where(down[:, :1] >= 0.0, 1.0, 0.0)
    return allowed, live, position


def rope_tables(position, heads, size, width):
    half = ROT // 2
    index = lax.broadcasted_iota(jnp.int32, (half, 1), 0).astype(F32)
    angle = jnp.exp(index * (-2.0 * math.log(10000.0) / ROT)) * position
    cosine = jnp.concatenate([jnp.cos(angle)] * (128 // half), axis=0).T
    sine = jnp.concatenate([jnp.sin(angle)] * (128 // half), axis=0).T
    lane = lax.broadcasted_iota(jnp.int32, (1, width), 1)
    part, dim = lane // size, lane % size
    value = part >= 3 * heads
    for head in range(heads):
        value = value | (part == 3 * head + 2)
    turned = jnp.logical_not(value) & (dim < ROT)
    low = turned & (dim < half)
    high = turned & (dim >= half)
    blocks = width // 128
    cosine = jnp.concatenate([cosine] * blocks, axis=1)
    sine = jnp.concatenate([sine] * blocks, axis=1)
    return (
        jnp.where(turned, cosine, 1.0),
        jnp.where(low, sine, 0.0),
        jnp.where(high, sine, 0.0),
    )


def turn(field, tables, sign):
    cosine, low, high = tables
    width = field.shape[1]
    ahead = pltpu.roll(field, width - ROT // 2, 1)
    behind = pltpu.roll(field, ROT // 2, 1)
    return field * cosine + sign * (behind * high - ahead * low)


def gelu_pair(expanded):
    cumulative = 0.5 * (1.0 + lax.erf(expanded * (1.0 / math.sqrt(2.0))))
    density = jnp.exp(-0.5 * expanded * expanded) * (1.0 / math.sqrt(2.0 * math.pi))
    return expanded * cumulative, cumulative + expanded * density


def ffn_block(normed_two, grad_out, expand, thresholds, contract):
    expanded = dot(normed_two, expand) + thresholds
    active, slope = gelu_pair(expanded)
    grad = dot_t(grad_out, contract) * slope
    return active.astype(BF16), grad


def attention_block(normed_one, grad_out, allowed, position, inlet_t, offsets, outlet, heads, size):
    n = normed_one.shape[0]
    columns = inlet_t.shape[0]
    width = -(-columns // 128) * 128
    tables = rope_tables(position, heads, size, width)
    projected = dot_t(normed_one, inlet_t) + offsets
    if width > columns:
        projected = jnp.concatenate([projected, jnp.zeros((n, width - columns), F32)], axis=1)
    turned = turn(projected, tables, 1.0).astype(BF16)
    attended_grad = dot_t(grad_out, outlet).astype(BF16)
    attended, grads = [], []
    for head in range(heads):
        at = 3 * head * size
        query = turned[:, at : at + size]
        key = turned[:, at + size : at + 2 * size]
        value = turned[:, at + 2 * size : at + 3 * size]
        back = attended_grad[:, head * size : (head + 1) * size]
        scores = jnp.where(allowed, dot_t(query, key) * 0.125, -jnp.inf)
        raised = jnp.exp(scores - jnp.max(scores, axis=-1, keepdims=True))
        weight = raised * (1.0 / jnp.sum(raised, axis=-1, keepdims=True))
        softmax = weight.astype(BF16)
        attended.append(dot(softmax, value).astype(BF16))
        prob_grad = dot_t(back, value)
        delta = jnp.sum(weight * prob_grad, axis=-1, keepdims=True)
        score_grad = (weight * (prob_grad - delta)).astype(BF16)
        grads.append(dot(score_grad, key) * 0.125)
        grads.append(dot_rows(score_grad, query) * 0.125)
        grads.append(dot_rows(softmax, back))
    if width > columns:
        grads.append(jnp.zeros((n, width - columns), F32))
    inlet_full = turn(jnp.concatenate(grads, axis=1), tables, -1.0)
    return jnp.concatenate(attended, axis=1), inlet_full


def flat(ref):
    rows = [ref[i : i + 1, :] for i in range(ref.shape[0])]
    return jnp.concatenate(rows, axis=1) if len(rows) > 1 else rows[0]


def folded(value):
    size = value.shape[0]
    return value.reshape(size // 128, 128) if size % 128 == 0 else value.reshape(1, size)


def label_row(seg_ref):
    return flat(seg_ref).astype(F32)


def live_column(seg_row):
    down = jnp.broadcast_to(seg_row, (128, seg_row.shape[1])).T
    return jnp.where(down[:, :1] >= 0.0, 1.0, 0.0)


def gather_kernel(tok_ref, cot_ref, seg_any, out_ref, seg_ref, sem, seg_sem):
    n = tok_ref.shape[0]
    labels = pltpu.make_async_copy(seg_any, seg_ref, seg_sem)
    labels.start()

    @pl.when(core_bit() == 0)
    def _():
        pltpu.make_async_copy(tok_ref, out_ref.at[0:n], sem).start()

    @pl.when(core_bit() != 0)
    def _():
        pltpu.make_async_copy(cot_ref, out_ref.at[0:n], sem).start()

    width = out_ref.shape[1]
    labels.wait()
    row = label_row(seg_ref)
    row = jnp.concatenate([row, jnp.zeros((1, width - n), F32)], axis=1)
    out_ref[n : n + 16] = jnp.broadcast_to(row, (16, width)).astype(BF16)
    pltpu.make_async_copy(tok_ref, out_ref.at[0:n], sem).wait()


def own_kernel(
    heads, size, n_dp, n_tensor,
    tok_any, cot_any, seg_ref, gain_one_ref, shift_one_ref, gain_two_ref, shift_two_ref, offsets_ref, thr_ref,
    inlet_any, outlet_any, expand_any, contract_any,
    tok_ref, cot_ref, inlet_ref, outlet_ref, expand_ref, contract_ref,
    away_ref, keep_ref, active_ref, back_ref, attended_ref, inlet_back_ref, tile_ref, one_ref, two_ref, out_ref,
    sems,
):
    copies = [
        pltpu.make_async_copy(a, b, sems.at[i])
        for i, (a, b) in enumerate(
            [(tok_any, tok_ref), (cot_any, cot_ref), (expand_any, expand_ref), (contract_any, contract_ref),
             (inlet_any, inlet_ref), (outlet_any, outlet_ref)]
        )
    ]
    for copy in copies:
        copy.start()
    seg_row = label_row(seg_ref)
    allowed, live, position = label_tables(seg_row)
    gain_one, shift_one = flat(gain_one_ref), flat(shift_one_ref)
    gain_two, shift_two = flat(gain_two_ref), flat(shift_two_ref)
    offsets = jnp.concatenate([offsets_ref[i : i + 1, :] for i in range(heads)], axis=1)
    thr = flat(thr_ref)
    copies[0].wait()
    scaled, inverse = norm_parts(tok_ref[...])
    normed_one = (scaled * gain_one + shift_one).astype(BF16)
    normed_two = (scaled * gain_two + shift_two).astype(BF16)
    copies[1].wait()
    grad_full = cot_ref[...].astype(F32) * live
    grad_out = grad_full.astype(BF16)
    put_left(normed_one, one_ref)
    put_left(normed_two, two_ref)
    put_left(grad_out, out_ref)
    copies[2].wait()
    copies[3].wait()
    active, expanded_grad = ffn_block(normed_two, grad_out, expand_ref[...], thr, contract_ref[...])
    expanded_back = expanded_grad.astype(BF16)
    copies[4].wait()
    copies[5].wait()
    attended, inlet_full = attention_block(
        normed_one, grad_out, allowed, position, inlet_ref[...], offsets, outlet_ref[...], heads, size
    )
    columns = inlet_ref.shape[0]
    inlet_back = inlet_full.astype(BF16)[:, :columns]
    active_ref[...] = active
    back_ref[...] = expanded_back
    attended_ref[...] = attended
    inlet_back_ref[...] = inlet_back
    branch = dot(attended, outlet_ref[...]) + dot(active, contract_ref[...])
    one_grad = dot(inlet_back, inlet_ref[...])
    two_grad = dot_t(expanded_back, expand_ref[...])
    lifted = one_grad * gain_one + two_grad * gain_two
    local = inverse * (
        lifted
        - jnp.mean(lifted, axis=-1, keepdims=True)
        - scaled * jnp.mean(lifted * scaled, axis=-1, keepdims=True)
    )
    core = core_bit()
    away_ref[...] = jnp.where(core == 0, local, branch).astype(BF16)
    keep_ref[...] = jnp.where(core == 0, branch, local)

    def total(field):
        return jnp.sum(field, axis=0, keepdims=True)

    everyone = jnp.concatenate(
        [total(one_grad * scaled), total(one_grad), total(two_grad * scaled), total(two_grad)], axis=0
    )
    bias = total(grad_full)
    hidden = total(expanded_grad)
    shares = total(inlet_full)
    block = tile_ref.shape[3]
    third = 3 * size // n_dp
    per_dp = hidden.shape[1] // n_dp
    tile_ref[...] = jnp.zeros_like(tile_ref)
    for d in range(n_dp):
        lanes = slice(d * block, (d + 1) * block)
        for t in range(n_tensor):
            tile_ref[d, t, 0:4] = everyone[:, lanes]

        def put(t, d=d, lanes=lanes):
            tile_ref[d, t, 4:5] = bias[:, lanes]
            tile_ref[d, t, 5:6, :per_dp] = hidden[:, d * per_dp : (d + 1) * per_dp]
            for head in range(heads):
                at = head * 3 * size + d * third
                tile_ref[d, t, 6:7, head * third : (head + 1) * third] = shares[:, at : at + third]

        put(lax.axis_index("tensor"))


def gather_bit():
    return lax.axis_index("dp") // 2 % 2


def first_bit():
    return lax.axis_index("dp") % 2


def core_bit():
    return lax.axis_index("tensor") % 2


def put_left(left, ref):
    ref[...] = left.T if ref.shape[0] != left.shape[0] else left


def left_shape(n, width, dests):
    return (width, n) if width // dests % 16 == 0 and width != n else (n, width)


def spread_rows(refs, dests):
    _, width = sorted(refs[0].shape)
    block = width // dests
    if refs[0].shape[0] == width:
        rows = []
        for flip in (1, 0):
            first = first_bit() if flip == 0 else 1 - first_bit()
            for rest in range(dests // 4):
                start = pl.multiple_of((4 * rest + 2 * gather_bit() + first) * block, 16)
                rows.append(jnp.concatenate([ref[pl.ds(start, block), :] for ref in refs], axis=1))
        return jnp.concatenate(rows, axis=0)
    half = dests // 4 * block
    row = lax.broadcasted_iota(jnp.int32, (2 * half, width), 0)
    col = lax.broadcasted_iota(jnp.int32, (2 * half, width), 1)
    kept = row >= half
    row = jnp.where(kept, row - half, row)
    first = jnp.where(kept, first_bit(), 1 - first_bit())
    want = row + (row // block) * 3 * block + (2 * gather_bit() + first) * block
    left = jnp.concatenate([ref[...] for ref in refs], axis=0)
    return dot_t(jnp.where(want == col, 1.0, 0.0).astype(BF16), left).astype(BF16)


def partner_inputs(got_ref, swap_ref, n):
    core = core_bit()
    got, swapped = got_ref[0:n], swap_ref[0:n]
    tok = jnp.where(core == 0, got, swapped)
    cot = jnp.where(core == 0, swapped, got)
    return tok, cot, got_ref[n : n + 1, :n].astype(F32)


def put_halves(product, send_ref, keep_ref):
    half = product.shape[0] // 2
    send_ref[...] = product[:half].astype(BF16)
    keep_ref[...] = product[half:]


def expand_kernel(
    dests,
    got_ref, swap_ref, two_ref, gain_ref, shift_ref, expand_ref, thr_ref, contract_ref, back_ref,
    send_ref, keep_ref, active_ref, grad_ref,
    left_ref,
):
    n = back_ref.shape[0]
    tok, cot, seg = partner_inputs(got_ref, swap_ref, n)
    scaled, _ = norm_parts(tok)
    normed = (scaled * flat(gain_ref) + flat(shift_ref)).astype(BF16)
    grad_out = (cot.astype(F32) * live_column(seg)).astype(BF16)
    grad_ref[...] = grad_out
    put_left(normed, left_ref)
    active, grad = ffn_block(normed, grad_out, expand_ref[...], flat(thr_ref), contract_ref[...])
    active_ref[...] = active
    right = jnp.concatenate([back_ref[...], grad.astype(BF16)], axis=0)
    put_halves(dot(spread_rows((two_ref, left_ref), dests), right), send_ref, keep_ref)


def contract_kernel(dests, grad_ref, out_ref, own_ref, active_ref, send_ref, keep_ref, left_ref):
    put_left(grad_ref[...], left_ref)
    right = jnp.concatenate([own_ref[...], active_ref[...]], axis=0)
    put_halves(dot(spread_rows((out_ref, left_ref), dests), right), send_ref, keep_ref)


def attention_kernel(
    heads, size, dests,
    got_ref, swap_ref, grad_ref, gain_ref, shift_ref, inlet_ref, offsets_ref, outlet_ref, attended_ref, inlet_back_ref,
    one_ref, out_ref, near_ref,
    send_ref, keep_ref,
    left_ref,
):
    n = attended_ref.shape[0]
    tok, _, seg = partner_inputs(got_ref, swap_ref, n)
    allowed, _, position = label_tables(seg)
    offsets = jnp.concatenate([offsets_ref[i : i + 1, :] for i in range(heads)], axis=1)
    scaled, _ = norm_parts(tok)
    normed = (scaled * flat(gain_ref) + flat(shift_ref)).astype(BF16)
    put_left(normed, left_ref)
    attended, inlet_full = attention_block(
        normed, grad_ref[...], allowed, position, inlet_ref[...], offsets, outlet_ref[...], heads, size
    )
    inlet_back = inlet_full.astype(BF16)[:, : inlet_ref.shape[0]]
    right = jnp.concatenate([inlet_back_ref[...], inlet_back], axis=0)
    first = dot(spread_rows((one_ref, left_ref), dests), right)
    right = jnp.concatenate([attended_ref[...], attended], axis=0)
    second = dot(spread_rows((out_ref, near_ref), dests), right)
    put_halves(jnp.concatenate([first, second], axis=1), send_ref, keep_ref)


def halve_kernel(step, keep_ref, got_ref, send_ref, left_ref):
    bit = jnp.where((lax.axis_index("dp") & step) != 0, 1, 0)
    for i in range(send_ref.shape[0]):
        away, stay = 2 * i + 1 - bit, 2 * i + bit
        send_ref[i] = (keep_ref[away] + got_ref[away].astype(F32)).astype(BF16)
        left_ref[i] = keep_ref[stay] + got_ref[stay].astype(F32)


def add_kernel(keep_ref, got_ref, out_ref):
    out_ref[...] = keep_ref[0] + got_ref[0].astype(F32)


def split_kernel(keep_ref, got_ref, inlet_ref, outlet_ref):
    total = keep_ref[0] + got_ref[0].astype(F32)
    columns = inlet_ref.shape[1]
    inlet_ref[...] = total[:, :columns]
    outlet_ref[...] = total[:, columns:].T


def part_kernel(keep_ref, got_ref, out_ref):
    out_ref[...] = (keep_ref[...].astype(F32) + got_ref[...].astype(F32)).astype(BF16)


def done_kernel(part_ref, got_ref, tok_ref, cot_ref, seg_ref, bias_ref, other_ref, out_ref):
    part = part_ref[...].astype(F32) + got_ref[...].astype(F32)
    shift = flat(bias_ref) + flat(other_ref)
    live = live_column(label_row(seg_ref))
    base = jnp.where(core_bit() == 0, tok_ref[...].astype(F32) + shift, cot_ref[...].astype(F32) * live)
    out_ref[...] = (base + part).astype(BF16)


def pair_kernel(own_ref, got_ref, mixed_ref, grad_ref):
    first = core_bit() == 0
    own, got = own_ref[...], got_ref[...]
    mixed_ref[...] = jnp.where(first, own, got)
    grad_ref[...] = jnp.where(first, got, own)


def small_kernel(heads, third, tile_ref, norms_ref, bias_ref, thr_ref, offsets_ref):
    total = tile_ref[0]
    for i in range(1, tile_ref.shape[0]):
        total = total + tile_ref[i]
    norms_ref[...] = total[0:4]
    bias_ref[...] = total[4:5]
    thr_ref[...] = total[5:6, : thr_ref.shape[1]]
    for head in range(heads):
        offsets_ref[head : head + 1] = total[6:7, head * third : (head + 1) * third]


def call(kernel, outs, args, flops=0, scratch=(), limit=VMEM_LIMIT, places="", results=""):
    kinds = {"v": pl.BlockSpec(memory_space=pltpu.VMEM), "a": pl.BlockSpec(memory_space=pltpu.HBM), "d": pl.BlockSpec()}
    places = places or "v" * len(args)
    results = results or "v" * len(outs)
    moved = sum(math.prod(s) * jnp.dtype(t).itemsize for s, t in outs)
    moved += sum(math.prod(a.shape) * a.dtype.itemsize for a in args)
    args = [pltpu.with_memory_space_constraint(a, pltpu.HBM) if k == "a" else a for a, k in zip(args, places)]
    return pl.pallas_call(
        kernel,
        out_shape=[jax.ShapeDtypeStruct(shape, dtype) for shape, dtype in outs],
        in_specs=[kinds[k] for k in places],
        out_specs=[kinds[k] for k in results],
        scratch_shapes=list(scratch),
        compiler_params=pltpu.CompilerParams(vmem_limit_bytes=limit),
        cost_estimate=pl.CostEstimate(flops=int(flops), bytes_accessed=moved, transcendentals=0),
    )(*args)


def swap(value, axis, count, bit):
    return lax.ppermute(value, axis, [(i, i ^ bit) for i in range(count)])


def step(n_dp, n_tensor, tokens, segments, first_gain, first_shift, second_gain, second_shift, inlet, offsets,
         outlet, outlet_bias, expand, thresholds, contract, contract_bias, cotangent):
    n, width = tokens.shape
    heads, size = offsets.shape[0], offsets.shape[1] // 3
    units = expand.shape[1]
    columns = inlet.shape[1]
    mine = outlet.shape[0]
    block = width // n_dp
    seg = folded(segments)
    gain_one, shift_one, gain_two, shift_two = map(folded, (first_gain, first_shift, second_gain, second_shift))
    thr = folded(thresholds)

    turned = left_shape(n, width, n_dp)

    payload, = call(
        gather_kernel, [((n + 16, width), BF16)], [tokens, cotangent, seg],
        scratch=[pltpu.VMEM(seg.shape, seg.dtype), pltpu.SemaphoreType.DMA, pltpu.SemaphoreType.DMA], places="aaa",
    )
    got = swap(payload, "dp", n_dp, 2)
    other = swap(got, "tensor", n_tensor, 1)

    (tok, cot, inlet_v, outlet_v, expand_v, contract_v, away, keep, active, back, attended, inlet_back, tile,
     one_t, two_t, out_t) = call(
        functools.partial(own_kernel, heads, size, n_dp, n_tensor),
        [(tokens.shape, BF16), (cotangent.shape, BF16), ((columns, width), BF16), (outlet.shape, BF16), (expand.shape, BF16),
         (contract.shape, BF16), ((n, width), BF16), ((n, width), F32), ((n, units), BF16), ((n, units), BF16),
         ((n, mine), BF16), ((n, columns), BF16), ((n_dp, n_tensor, 8, block), F32),
         (turned, BF16), (turned, BF16), (turned, BF16)],
        [tokens, cotangent, seg, gain_one, shift_one, gain_two, shift_two, offsets, thr, inlet.T, outlet, expand, contract],
        flops=6e9, scratch=[pltpu.SemaphoreType.DMA((6,))], places="aavvvvvvvaaaa",
    )
    half = n_dp // 4 * block
    left = [pltpu.VMEM(turned, BF16)]

    expand_send, expand_keep, active_near, grad_near = call(
        functools.partial(expand_kernel, n_dp),
        [((half, units), BF16), ((half, units), F32), ((n, units), BF16), ((n, width), BF16)],
        [got, other, two_t, gain_two, shift_two, expand_v, thr, contract_v, back],
        flops=3e9, scratch=left,
    )
    expand_got = swap(expand_send, "dp", n_dp, 1)
    contract_send, contract_keep, near_t = call(
        functools.partial(contract_kernel, n_dp),
        [((half, units), BF16), ((half, units), F32), (turned, BF16)],
        [grad_near, out_t, active, active_near],
        flops=1e9,
    )
    contract_got = swap(contract_send, "dp", n_dp, 1)
    tail_send, tail_keep = call(
        functools.partial(attention_kernel, heads, size, n_dp),
        [((half, columns + mine), BF16), ((half, columns + mine), F32)],
        [got, other, grad_near, gain_one, shift_one, inlet_v, offsets, outlet_v, attended, inlet_back, one_t, out_t, near_t],
        flops=5e9, scratch=left,
    )
    tail_got = swap(tail_send, "dp", n_dp, 1)

    part = keep
    near = swap(away, "tensor", n_tensor, 1)
    part, = call(part_kernel, [((n, width), BF16)], [keep, near], flops=1e6)
    bit = 2
    while 2 * bit < n_tensor:
        part, = call(part_kernel, [((n, width), BF16)], [part, swap(part, "tensor", n_tensor, bit)])
        bit *= 2
    far = swap(part, "tensor", n_tensor, bit)
    done, = call(
        done_kernel, [((n, width), BF16)],
        [part, far, tok, cot, seg, folded(outlet_bias), folded(contract_bias)], flops=1e6,
    )
    paired = swap(done, "tensor", n_tensor, 1)
    mixed, input_grad = call(pair_kernel, [((n, width), BF16)] * 2, [done, paired], results="dd")

    tile = lax.all_to_all(tile.reshape(n_dp * n_tensor, 8, block), ("dp", "tensor"), 0, 0, tiled=True)
    third = offsets.shape[1] // n_dp
    norm_grads, bias_grad, thr_grad, offsets_grad = call(
        functools.partial(small_kernel, heads, third),
        [((4, block), F32), ((1, block), F32), ((1, units // n_dp), F32), ((heads, third), F32)], [tile], results="dddd",
    )

    def reduce(kept, arrived):
        columns_here = kept.shape[1]
        kept = kept.reshape(-1, block, columns_here)
        arrived = arrived.reshape(-1, block, columns_here)
        bit = 4
        while bit < n_dp:
            rest = kept.shape[0] // 2
            shape = (rest, block, columns_here)
            away, kept = call(
                functools.partial(halve_kernel, bit), [(shape, BF16), (shape, F32)], [kept, arrived],
                flops=1e6,
            )
            arrived = swap(away, "dp", n_dp, bit)
            bit *= 2
        return kept, arrived

    expand_grad, = call(add_kernel, [((block, units), F32)], reduce(expand_keep, expand_got), results="d")
    contract_grad, = call(add_kernel, [((block, units), F32)], reduce(contract_keep, contract_got), results="d")
    inlet_grad, outlet_grad = call(
        split_kernel, [((block, columns), F32), ((mine, block), F32)],
        reduce(tail_keep, tail_got), results="dd",
    )
    return (
        mixed, input_grad, inlet_grad, offsets_grad, outlet_grad, expand_grad, thr_grad, contract_grad.T,
        bias_grad.reshape(block), norm_grads,
    )


def solution(mesh):
    placed = (
        P("dp", None), P("dp"), P(), P(), P(), P(), P(None, "tensor"), P("tensor", None), P("tensor", None),
        P(), P(None, "tensor"), P("tensor"), P("tensor", None), P(), P("dp", None),
    )
    return jax.shard_map(
        functools.partial(step, mesh.shape["dp"], mesh.shape["tensor"]),
        mesh=mesh,
        in_specs=placed,
        out_specs=(
            P("dp", None), P("dp", None), P("dp", "tensor"), P("tensor", "dp"), P("tensor", "dp"),
            P("dp", "tensor"), P("tensor", "dp"), P("tensor", "dp"), P("dp"), P(None, "dp"),
        ),
        check_vma=False,
    )
```

```python
import functools
import math

import jax
import jax.numpy as jnp
from jax import lax
from jax.experimental import pallas as pl
from jax.experimental.pallas import tpu as pltpu
from jax.sharding import PartitionSpec as P


ROT = 16
EPS = 1e-05
F32 = jnp.float32
BF16 = jnp.bfloat16
MIB = 1024 * 1024
VMEM_LIMIT = 32 * MIB


def dot(a, b):
    return jnp.dot(a, b, preferred_element_type=F32)


def dot_t(a, b):
    return lax.dot_general(a, b, (((1,), (1,)), ((), ())), preferred_element_type=F32)


def dot_rows(a, b):
    return lax.dot_general(a, b, (((0,), (0,)), ((), ())), preferred_element_type=F32)


def norm_parts(tok):
    x = tok.astype(F32)
    center = x - jnp.mean(x, axis=-1, keepdims=True)
    inverse = lax.rsqrt(jnp.mean(center * center, axis=-1, keepdims=True) + EPS)
    return center * inverse, inverse


def label_tables(seg_row):
    n = seg_row.shape[1]
    across = jnp.broadcast_to(seg_row, (n, n))
    down = across.T
    row = lax.broadcasted_iota(jnp.int32, (n, n), 0)
    col = lax.broadcasted_iota(jnp.int32, (n, n), 1)
    same = across == down
    allowed = same & (col <= row)
    position = jnp.sum(jnp.where(same & (row <= col), 1.0, 0.0), axis=0, keepdims=True) - 1.0
    live = jnp.where(down[:, :1] >= 0.0, 1.0, 0.0)
    return allowed, live, position


def rope_tables(position, heads, size, width):
    half = ROT // 2
    index = lax.broadcasted_iota(jnp.int32, (half, 1), 0).astype(F32)
    angle = jnp.exp(index * (-2.0 * math.log(10000.0) / ROT)) * position
    cosine = jnp.concatenate([jnp.cos(angle)] * (128 // half), axis=0).T
    sine = jnp.concatenate([jnp.sin(angle)] * (128 // half), axis=0).T
    lane = lax.broadcasted_iota(jnp.int32, (1, width), 1)
    part, dim = lane // size, lane % size
    value = part >= 3 * heads
    for head in range(heads):
        value = value | (part == 3 * head + 2)
    turned = jnp.logical_not(value) & (dim < ROT)
    low = turned & (dim < half)
    high = turned & (dim >= half)
    blocks = width // 128
    cosine = jnp.concatenate([cosine] * blocks, axis=1)
    sine = jnp.concatenate([sine] * blocks, axis=1)
    return (
        jnp.where(turned, cosine, 1.0),
        jnp.where(low, sine, 0.0),
        jnp.where(high, sine, 0.0),
    )


def turn(field, tables, sign):
    cosine, low, high = tables
    width = field.shape[1]
    ahead = pltpu.roll(field, width - ROT // 2, 1)
    behind = pltpu.roll(field, ROT // 2, 1)
    return field * cosine + sign * (behind * high - ahead * low)


def gelu_pair(expanded):
    cumulative = 0.5 * (1.0 + lax.erf(expanded * (1.0 / math.sqrt(2.0))))
    density = jnp.exp(-0.5 * expanded * expanded) * (1.0 / math.sqrt(2.0 * math.pi))
    return expanded * cumulative, cumulative + expanded * density


def ffn_block(normed_two, grad_out, expand, thresholds, contract):
    expanded = dot(normed_two, expand) + thresholds
    active, slope = gelu_pair(expanded)
    grad = dot_t(grad_out, contract) * slope
    return active.astype(BF16), grad


def attention_block(normed_one, grad_out, allowed, position, inlet_t, offsets, outlet, heads, size):
    n = normed_one.shape[0]
    columns = inlet_t.shape[0]
    width = -(-columns // 128) * 128
    tables = rope_tables(position, heads, size, width)
    projected = dot_t(normed_one, inlet_t) + offsets
    if width > columns:
        projected = jnp.concatenate([projected, jnp.zeros((n, width - columns), F32)], axis=1)
    turned = turn(projected, tables, 1.0).astype(BF16)
    attended_grad = dot_t(grad_out, outlet).astype(BF16)
    attended, grads = [], []
    for head in range(heads):
        at = 3 * head * size
        query = turned[:, at : at + size]
        key = turned[:, at + size : at + 2 * size]
        value = turned[:, at + 2 * size : at + 3 * size]
        back = attended_grad[:, head * size : (head + 1) * size]
        scores = jnp.where(allowed, dot_t(query, key) * 0.125, -jnp.inf)
        raised = jnp.exp(scores - jnp.max(scores, axis=-1, keepdims=True))
        weight = raised * (1.0 / jnp.sum(raised, axis=-1, keepdims=True))
        softmax = weight.astype(BF16)
        attended.append(dot(softmax, value).astype(BF16))
        prob_grad = dot_t(back, value)
        delta = jnp.sum(weight * prob_grad, axis=-1, keepdims=True)
        score_grad = (weight * (prob_grad - delta)).astype(BF16)
        grads.append(dot(score_grad, key) * 0.125)
        grads.append(dot_rows(score_grad, query) * 0.125)
        grads.append(dot_rows(softmax, back))
    if width > columns:
        grads.append(jnp.zeros((n, width - columns), F32))
    inlet_full = turn(jnp.concatenate(grads, axis=1), tables, -1.0)
    return jnp.concatenate(attended, axis=1), inlet_full


def flat(ref):
    rows = [ref[i : i + 1, :] for i in range(ref.shape[0])]
    return jnp.concatenate(rows, axis=1) if len(rows) > 1 else rows[0]


def folded(value):
    size = value.shape[0]
    return value.reshape(size // 128, 128) if size % 128 == 0 else value.reshape(1, size)


def label_row(seg_ref):
    return flat(seg_ref).astype(F32)


def live_column(seg_row):
    down = jnp.broadcast_to(seg_row, (128, seg_row.shape[1])).T
    return jnp.where(down[:, :1] >= 0.0, 1.0, 0.0)


def gather_kernel(tok_ref, cot_ref, seg_any, out_ref, seg_ref, sem, seg_sem):
    n = tok_ref.shape[0]
    labels = pltpu.make_async_copy(seg_any, seg_ref, seg_sem)
    labels.start()

    @pl.when(core_bit() == 0)
    def _():
        pltpu.make_async_copy(tok_ref, out_ref.at[0:n], sem).start()

    @pl.when(core_bit() != 0)
    def _():
        pltpu.make_async_copy(cot_ref, out_ref.at[0:n], sem).start()

    width = out_ref.shape[1]
    labels.wait()
    row = label_row(seg_ref)
    row = jnp.concatenate([row, jnp.zeros((1, width - n), F32)], axis=1)
    out_ref[n : n + 16] = jnp.broadcast_to(row, (16, width)).astype(BF16)
    pltpu.make_async_copy(tok_ref, out_ref.at[0:n], sem).wait()


def own_kernel(
    heads, size, n_dp, n_tensor,
    tok_any, cot_any, seg_ref, gain_one_ref, shift_one_ref, gain_two_ref, shift_two_ref, offsets_ref, thr_ref,
    inlet_any, outlet_any, expand_any, contract_any,
    tok_ref, cot_ref, inlet_ref, outlet_ref, expand_ref, contract_ref,
    away_ref, keep_ref, active_ref, back_ref, attended_ref, inlet_back_ref, tile_ref, one_ref, two_ref, out_ref,
    sems,
):
    copies = [
        pltpu.make_async_copy(a, b, sems.at[i])
        for i, (a, b) in enumerate(
            [(tok_any, tok_ref), (cot_any, cot_ref), (expand_any, expand_ref), (contract_any, contract_ref),
             (inlet_any, inlet_ref), (outlet_any, outlet_ref)]
        )
    ]
    for copy in copies:
        copy.start()
    seg_row = label_row(seg_ref)
    allowed, live, position = label_tables(seg_row)
    gain_one, shift_one = flat(gain_one_ref), flat(shift_one_ref)
    gain_two, shift_two = flat(gain_two_ref), flat(shift_two_ref)
    offsets = jnp.concatenate([offsets_ref[i : i + 1, :] for i in range(heads)], axis=1)
    thr = flat(thr_ref)
    copies[0].wait()
    scaled, inverse = norm_parts(tok_ref[...])
    normed_one = (scaled * gain_one + shift_one).astype(BF16)
    normed_two = (scaled * gain_two + shift_two).astype(BF16)
    copies[1].wait()
    grad_full = cot_ref[...].astype(F32) * live
    grad_out = grad_full.astype(BF16)
    put_left(normed_one, one_ref)
    put_left(normed_two, two_ref)
    put_left(grad_out, out_ref)
    copies[2].wait()
    copies[3].wait()
    active, expanded_grad = ffn_block(normed_two, grad_out, expand_ref[...], thr, contract_ref[...])
    expanded_back = expanded_grad.astype(BF16)
    copies[4].wait()
    copies[5].wait()
    attended, inlet_full = attention_block(
        normed_one, grad_out, allowed, position, inlet_ref[...], offsets, outlet_ref[...], heads, size
    )
    columns = inlet_ref.shape[0]
    inlet_back = inlet_full.astype(BF16)[:, :columns]
    active_ref[...] = active
    back_ref[...] = expanded_back
    attended_ref[...] = attended
    inlet_back_ref[...] = inlet_back
    branch = dot(attended, outlet_ref[...]) + dot(active, contract_ref[...])
    one_grad = dot(inlet_back, inlet_ref[...])
    two_grad = dot_t(expanded_back, expand_ref[...])
    lifted = one_grad * gain_one + two_grad * gain_two
    local = inverse * (
        lifted
        - jnp.mean(lifted, axis=-1, keepdims=True)
        - scaled * jnp.mean(lifted * scaled, axis=-1, keepdims=True)
    )
    core = core_bit()
    away_ref[...] = jnp.where(core == 0, local, branch).astype(BF16)
    keep_ref[...] = jnp.where(core == 0, branch, local)

    def total(field):
        return jnp.sum(field, axis=0, keepdims=True)

    everyone = jnp.concatenate(
        [total(one_grad * scaled), total(one_grad), total(two_grad * scaled), total(two_grad)], axis=0
    )
    bias = total(grad_full)
    hidden = total(expanded_grad)
    shares = total(inlet_full)
    block = tile_ref.shape[3]
    third = 3 * size // n_dp
    per_dp = hidden.shape[1] // n_dp
    for d in range(n_dp):
        lanes = slice(d * block, (d + 1) * block)
        local = hidden[:, d * per_dp : (d + 1) * per_dp]
        if per_dp < block:
            local = jnp.concatenate([local, jnp.zeros((1, block - per_dp), F32)], axis=1)
        cut = [shares[:, h * 3 * size + d * third : h * 3 * size + (d + 1) * third] for h in range(heads)]
        if heads * third < block:
            cut.append(jnp.zeros((1, block - heads * third), F32))
        mine = jnp.concatenate([bias[:, lanes], local, jnp.concatenate(cut, axis=1), jnp.zeros((1, block), F32)], axis=0)
        for t in range(n_tensor):
            here = jnp.where(lax.axis_index("tensor") == t, mine, 0.0)
            tile_ref[d, t] = jnp.concatenate([everyone[:, lanes], here], axis=0).astype(BF16)


def bit_of(bit):
    return lax.axis_index("dp") // bit % 2


def core_bit():
    return lax.axis_index("tensor") % 2


def other_bits(dests, first):
    return [1 << i for i in range(12) if 1 << i < dests and 1 << i not in (2, first)]


def dest_order(dests, first):
    bits = other_bits(dests, first)
    return [sum(bit for i, bit in enumerate(bits) if rest >> i & 1) for rest in range(1 << len(bits))]


def put_left(left, ref):
    ref[...] = left.T if ref.shape[0] != left.shape[0] else left


def left_shape(n, width, dests):
    return (width, n) if width // dests % 16 == 0 and width != n else (n, width)


def spread_rows(refs, dests, first):
    _, width = sorted(refs[0].shape)
    block = width // dests
    numbers = dest_order(dests, first)
    if refs[0].shape[0] == width:
        rows = []
        for flip in (1, 0):
            side = bit_of(first) if flip == 0 else 1 - bit_of(first)
            for number in numbers:
                start = pl.multiple_of((number + 2 * bit_of(2) + first * side) * block, 16)
                rows.append(jnp.concatenate([ref[pl.ds(start, block), :] for ref in refs], axis=1))
        return jnp.concatenate(rows, axis=0)
    half = len(numbers) * block
    row = lax.broadcasted_iota(jnp.int32, (2 * half, width), 0)
    col = lax.broadcasted_iota(jnp.int32, (2 * half, width), 1)
    kept = row >= half
    row = jnp.where(kept, row - half, row)
    side = jnp.where(kept, bit_of(first), 1 - bit_of(first))
    want = row + (2 * bit_of(2) + first * side) * block
    for place, number in enumerate(numbers):
        inside = (row >= place * block) & (row < (place + 1) * block)
        want = want + jnp.where(inside, (number - place) * block, 0)
    left = jnp.concatenate([ref[...] for ref in refs], axis=0)
    return dot_t(jnp.where(want == col, 1.0, 0.0).astype(BF16), left).astype(BF16)


def partner_inputs(got_ref, swap_ref, n):
    core = core_bit()
    got, swapped = got_ref[0:n], swap_ref[0:n]
    tok = jnp.where(core == 0, got, swapped)
    cot = jnp.where(core == 0, swapped, got)
    return tok, cot, got_ref[n : n + 1, :n].astype(F32)


def put_halves(product, send_ref, keep_ref):
    half = product.shape[0] // 2
    send_ref[...] = product[:half].astype(BF16)
    keep_ref[...] = product[half:]


def expand_kernel(
    dests,
    got_ref, swap_ref, two_ref, gain_ref, shift_ref, expand_ref, thr_ref, contract_ref, back_ref,
    send_ref, keep_ref, active_ref, grad_ref,
    left_ref,
):
    n = back_ref.shape[0]
    tok, cot, seg = partner_inputs(got_ref, swap_ref, n)
    scaled, _ = norm_parts(tok)
    normed = (scaled * flat(gain_ref) + flat(shift_ref)).astype(BF16)
    grad_out = (cot.astype(F32) * live_column(seg)).astype(BF16)
    grad_ref[...] = grad_out
    put_left(normed, left_ref)
    active, grad = ffn_block(normed, grad_out, expand_ref[...], flat(thr_ref), contract_ref[...])
    active_ref[...] = active
    right = jnp.concatenate([back_ref[...], grad.astype(BF16)], axis=0)
    put_halves(dot(spread_rows((two_ref, left_ref), dests, 1), right), send_ref, keep_ref)


def contract_kernel(
    dests, firsts, grad_ref, out_ref, own_ref, active_ref, send_a_ref, keep_a_ref, send_b_ref, keep_b_ref, left_ref
):
    put_left(grad_ref[...], left_ref)
    right = jnp.concatenate([own_ref[...], active_ref[...]], axis=0)
    split = send_a_ref.shape[1]
    put_halves(dot(spread_rows((out_ref, left_ref), dests, firsts[0]), right[:, :split]), send_a_ref, keep_a_ref)
    put_halves(dot(spread_rows((out_ref, left_ref), dests, firsts[1]), right[:, split:]), send_b_ref, keep_b_ref)


def attention_kernel(
    heads, size, dests,
    got_ref, swap_ref, grad_ref, gain_ref, shift_ref, inlet_ref, offsets_ref, outlet_ref, attended_ref, inlet_back_ref,
    one_ref, out_ref, near_ref,
    send_ref, keep_ref,
    left_ref,
):
    n = attended_ref.shape[0]
    tok, _, seg = partner_inputs(got_ref, swap_ref, n)
    allowed, _, position = label_tables(seg)
    offsets = jnp.concatenate([offsets_ref[i : i + 1, :] for i in range(heads)], axis=1)
    scaled, _ = norm_parts(tok)
    normed = (scaled * flat(gain_ref) + flat(shift_ref)).astype(BF16)
    put_left(normed, left_ref)
    attended, inlet_full = attention_block(
        normed, grad_ref[...], allowed, position, inlet_ref[...], offsets, outlet_ref[...], heads, size
    )
    inlet_back = inlet_full.astype(BF16)[:, : inlet_ref.shape[0]]
    right = jnp.concatenate([inlet_back_ref[...], inlet_back], axis=0)
    first = dot(spread_rows((one_ref, left_ref), dests, 1), right)
    right = jnp.concatenate([attended_ref[...], attended], axis=0)
    second = dot(spread_rows((out_ref, near_ref), dests, 1), right)
    put_halves(jnp.concatenate([first, second], axis=1), send_ref, keep_ref)


def halve_kernel(step, keep_ref, got_ref, send_ref, left_ref):
    bit = bit_of(step)
    for i in range(send_ref.shape[0]):
        away, stay = 2 * i + 1 - bit, 2 * i + bit
        send_ref[i] = (keep_ref[away] + got_ref[away].astype(F32)).astype(BF16)
        left_ref[i] = keep_ref[stay] + got_ref[stay].astype(F32)


def add_kernel(*refs):
    out_ref, at = refs[-1], 0
    for keep_ref, got_ref in zip(refs[:-1:2], refs[1:-1:2]):
        columns = keep_ref.shape[2]
        out_ref[:, at : at + columns] = keep_ref[0] + got_ref[0].astype(F32)
        at += columns


def split_kernel(keep_ref, got_ref, inlet_ref, outlet_ref):
    total = keep_ref[0] + got_ref[0].astype(F32)
    columns = inlet_ref.shape[1]
    inlet_ref[...] = total[:, :columns]
    outlet_ref[...] = total[:, columns:].T


def part_kernel(keep_ref, got_ref, out_ref):
    out_ref[...] = (keep_ref[...].astype(F32) + got_ref[...].astype(F32)).astype(BF16)


def done_kernel(part_ref, got_ref, tok_ref, cot_ref, seg_ref, bias_ref, other_ref, out_ref):
    part = part_ref[...].astype(F32) + got_ref[...].astype(F32)
    shift = flat(bias_ref) + flat(other_ref)
    live = live_column(label_row(seg_ref))
    base = jnp.where(core_bit() == 0, tok_ref[...].astype(F32) + shift, cot_ref[...].astype(F32) * live)
    out_ref[...] = (base + part).astype(BF16)


def pair_kernel(own_ref, got_ref, mixed_ref, grad_ref):
    first = core_bit() == 0
    own, got = own_ref[...], got_ref[...]
    mixed_ref[...] = jnp.where(first, own, got)
    grad_ref[...] = jnp.where(first, got, own)


def small_kernel(heads, third, tile_ref, norms_ref, bias_ref, thr_ref, offsets_ref):
    total = tile_ref[0].astype(F32)
    for i in range(1, tile_ref.shape[0]):
        total = total + tile_ref[i].astype(F32)
    norms_ref[...] = total[0:4]
    bias_ref[...] = total[4:5]
    thr_ref[...] = total[5:6, : thr_ref.shape[1]]
    for head in range(heads):
        offsets_ref[head : head + 1] = total[6:7, head * third : (head + 1) * third]


def call(kernel, outs, args, flops=0, scratch=(), limit=VMEM_LIMIT, places="", results=""):
    kinds = {"v": pl.BlockSpec(memory_space=pltpu.VMEM), "a": pl.BlockSpec(memory_space=pltpu.HBM), "d": pl.BlockSpec()}
    places = places or "v" * len(args)
    results = results or "v" * len(outs)
    moved = sum(math.prod(s) * jnp.dtype(t).itemsize for s, t in outs)
    moved += sum(math.prod(a.shape) * a.dtype.itemsize for a in args)
    args = [pltpu.with_memory_space_constraint(a, pltpu.HBM) if k == "a" else a for a, k in zip(args, places)]
    return pl.pallas_call(
        kernel,
        out_shape=[jax.ShapeDtypeStruct(shape, dtype) for shape, dtype in outs],
        in_specs=[kinds[k] for k in places],
        out_specs=[kinds[k] for k in results],
        scratch_shapes=list(scratch),
        compiler_params=pltpu.CompilerParams(vmem_limit_bytes=limit),
        cost_estimate=pl.CostEstimate(flops=int(flops), bytes_accessed=moved, transcendentals=0),
    )(*args)


def swap(value, axis, count, bit):
    return lax.ppermute(value, axis, [(i, i ^ bit) for i in range(count)])


def step(n_dp, n_tensor, tokens, segments, first_gain, first_shift, second_gain, second_shift, inlet, offsets,
         outlet, outlet_bias, expand, thresholds, contract, contract_bias, cotangent):
    n, width = tokens.shape
    heads, size = offsets.shape[0], offsets.shape[1] // 3
    units = expand.shape[1]
    columns = inlet.shape[1]
    mine = outlet.shape[0]
    block = width // n_dp
    seg = folded(segments)
    gain_one, shift_one, gain_two, shift_two = map(folded, (first_gain, first_shift, second_gain, second_shift))
    thr = folded(thresholds)

    turned = left_shape(n, width, n_dp)

    payload, = call(
        gather_kernel, [((n + 16, width), BF16)], [tokens, cotangent, seg],
        scratch=[pltpu.VMEM(seg.shape, seg.dtype), pltpu.SemaphoreType.DMA, pltpu.SemaphoreType.DMA], places="aaa",
    )
    got = swap(payload, "dp", n_dp, 2)
    other = swap(got, "tensor", n_tensor, 1)

    (tok, cot, inlet_v, outlet_v, expand_v, contract_v, away, keep, active, back, attended, inlet_back, tile,
     one_t, two_t, out_t) = call(
        functools.partial(own_kernel, heads, size, n_dp, n_tensor),
        [(tokens.shape, BF16), (cotangent.shape, BF16), ((columns, width), BF16), (outlet.shape, BF16), (expand.shape, BF16),
         (contract.shape, BF16), ((n, width), BF16), ((n, width), F32), ((n, units), BF16), ((n, units), BF16),
         ((n, mine), BF16), ((n, columns), BF16), ((n_dp, n_tensor, 8, block), BF16),
         (turned, BF16), (turned, BF16), (turned, BF16)],
        [tokens, cotangent, seg, gain_one, shift_one, gain_two, shift_two, offsets, thr, inlet.T, outlet, expand, contract],
        flops=6e9, scratch=[pltpu.SemaphoreType.DMA((6,))], places="aavvvvvvvaaaa",
    )
    half = n_dp // 4 * block
    left = [pltpu.VMEM(turned, BF16)]

    expand_send, expand_keep, active_near, grad_near = call(
        functools.partial(expand_kernel, n_dp),
        [((half, units), BF16), ((half, units), F32), ((n, units), BF16), ((n, width), BF16)],
        [got, other, two_t, gain_two, shift_two, expand_v, thr, contract_v, back],
        flops=3e9, scratch=left,
    )
    expand_got = swap(expand_send, "dp", n_dp, 1)
    far_first = 4 if n_dp > 4 else 1
    part_units = units // 2
    early_send, early_keep, late_send, late_keep, near_t = call(
        functools.partial(contract_kernel, n_dp, (far_first, 1)),
        [((half, part_units), BF16), ((half, part_units), F32), ((half, units - part_units), BF16),
         ((half, units - part_units), F32), (turned, BF16)],
        [grad_near, out_t, active, active_near],
        flops=1e9,
    )
    early_got = swap(early_send, "dp", n_dp, far_first)
    late_got = swap(late_send, "dp", n_dp, 1)
    tail_send, tail_keep = call(
        functools.partial(attention_kernel, heads, size, n_dp),
        [((half, columns + mine), BF16), ((half, columns + mine), F32)],
        [got, other, grad_near, gain_one, shift_one, inlet_v, offsets, outlet_v, attended, inlet_back, one_t, out_t, near_t],
        flops=5e9, scratch=left,
    )
    tail_got = swap(tail_send, "dp", n_dp, 1)

    part = keep
    near = swap(away, "tensor", n_tensor, 1)
    part, = call(part_kernel, [((n, width), BF16)], [keep, near], flops=1e6)
    bit = 2
    while 2 * bit < n_tensor:
        part, = call(part_kernel, [((n, width), BF16)], [part, swap(part, "tensor", n_tensor, bit)])
        bit *= 2
    far = swap(part, "tensor", n_tensor, bit)
    done, = call(
        done_kernel, [((n, width), BF16)],
        [part, far, tok, cot, seg, folded(outlet_bias), folded(contract_bias)], flops=1e6,
    )
    paired = swap(done, "tensor", n_tensor, 1)
    mixed, input_grad = call(pair_kernel, [((n, width), BF16)] * 2, [done, paired], results="dd")

    tile = lax.all_to_all(tile.reshape(n_dp * n_tensor, 8, block), ("dp", "tensor"), 0, 0, tiled=True)
    third = offsets.shape[1] // n_dp
    norm_grads, bias_grad, thr_grad, offsets_grad = call(
        functools.partial(small_kernel, heads, third),
        [((4, block), F32), ((1, block), F32), ((1, units // n_dp), F32), ((heads, third), F32)], [tile], results="dddd",
    )

    def reduce(kept, arrived, first):
        columns_here = kept.shape[1]
        kept = kept.reshape(-1, block, columns_here)
        arrived = arrived.reshape(-1, block, columns_here)
        for bit in other_bits(n_dp, first):
            rest = kept.shape[0] // 2
            shape = (rest, block, columns_here)
            away, kept = call(
                functools.partial(halve_kernel, bit), [(shape, BF16), (shape, F32)], [kept, arrived], flops=1e6
            )
            arrived = swap(away, "dp", n_dp, bit)
        return [kept, arrived]

    expand_grad, = call(add_kernel, [((block, units), F32)], reduce(expand_keep, expand_got, 1), results="d")
    contract_grad, = call(
        add_kernel, [((block, units), F32)],
        reduce(early_keep, early_got, far_first) + reduce(late_keep, late_got, 1), results="d",
    )
    inlet_grad, outlet_grad = call(
        split_kernel, [((block, columns), F32), ((mine, block), F32)],
        reduce(tail_keep, tail_got, 1), results="dd",
    )
    return (
        mixed, input_grad, inlet_grad, offsets_grad, outlet_grad, expand_grad, thr_grad, contract_grad.T,
        bias_grad.reshape(block), norm_grads,
    )


def solution(mesh):
    placed = (
        P("dp", None), P("dp"), P(), P(), P(), P(), P(None, "tensor"), P("tensor", None), P("tensor", None),
        P(), P(None, "tensor"), P("tensor"), P("tensor", None), P(), P("dp", None),
    )
    return jax.shard_map(
        functools.partial(step, mesh.shape["dp"], mesh.shape["tensor"]),
        mesh=mesh,
        in_specs=placed,
        out_specs=(
            P("dp", None), P("dp", None), P("dp", "tensor"), P("tensor", "dp"), P("tensor", "dp"),
            P("dp", "tensor"), P("tensor", "dp"), P("tensor", "dp"), P("dp"), P(None, "dp"),
        ),
        check_vma=False,
    )
```

```python
import functools
import math

import jax
import jax.numpy as jnp
from jax import lax
from jax.experimental import pallas as pl
from jax.experimental.pallas import tpu as pltpu
from jax.sharding import PartitionSpec as P


ROT = 16
EPS = 1e-05
F32 = jnp.float32
BF16 = jnp.bfloat16
MIB = 1024 * 1024
VMEM_LIMIT = 32 * MIB


def dot(a, b):
    return jnp.dot(a, b, preferred_element_type=F32)


def dot_t(a, b):
    return lax.dot_general(a, b, (((1,), (1,)), ((), ())), preferred_element_type=F32)


def dot_rows(a, b):
    return lax.dot_general(a, b, (((0,), (0,)), ((), ())), preferred_element_type=F32)


def norm_parts(tok):
    x = tok.astype(F32)
    center = x - jnp.mean(x, axis=-1, keepdims=True)
    inverse = lax.rsqrt(jnp.mean(center * center, axis=-1, keepdims=True) + EPS)
    return center * inverse, inverse


def label_tables(seg_row):
    n = seg_row.shape[1]
    across = jnp.broadcast_to(seg_row, (n, n))
    down = across.T
    row = lax.broadcasted_iota(jnp.int32, (n, n), 0)
    col = lax.broadcasted_iota(jnp.int32, (n, n), 1)
    same = across == down
    allowed = same & (col <= row)
    position = jnp.sum(jnp.where(same & (row <= col), 1.0, 0.0), axis=0, keepdims=True) - 1.0
    live = jnp.where(down[:, :1] >= 0.0, 1.0, 0.0)
    return allowed, live, position


def rope_tables(position, heads, size, width):
    half = ROT // 2
    index = lax.broadcasted_iota(jnp.int32, (half, 1), 0).astype(F32)
    angle = jnp.exp(index * (-2.0 * math.log(10000.0) / ROT)) * position
    cosine = jnp.concatenate([jnp.cos(angle)] * (128 // half), axis=0).T
    sine = jnp.concatenate([jnp.sin(angle)] * (128 // half), axis=0).T
    lane = lax.broadcasted_iota(jnp.int32, (1, width), 1)
    part, dim = lane // size, lane % size
    value = part >= 3 * heads
    for head in range(heads):
        value = value | (part == 3 * head + 2)
    turned = jnp.logical_not(value) & (dim < ROT)
    low = turned & (dim < half)
    high = turned & (dim >= half)
    blocks = width // 128
    cosine = jnp.concatenate([cosine] * blocks, axis=1)
    sine = jnp.concatenate([sine] * blocks, axis=1)
    return (
        jnp.where(turned, cosine, 1.0),
        jnp.where(low, sine, 0.0),
        jnp.where(high, sine, 0.0),
    )


def turn(field, tables, sign):
    cosine, low, high = tables
    width = field.shape[1]
    ahead = pltpu.roll(field, width - ROT // 2, 1)
    behind = pltpu.roll(field, ROT // 2, 1)
    return field * cosine + sign * (behind * high - ahead * low)


def gelu_pair(expanded):
    cumulative = 0.5 * (1.0 + lax.erf(expanded * (1.0 / math.sqrt(2.0))))
    density = jnp.exp(-0.5 * expanded * expanded) * (1.0 / math.sqrt(2.0 * math.pi))
    return expanded * cumulative, cumulative + expanded * density


def ffn_block(normed_two, grad_out, expand, thresholds, contract):
    expanded = dot(normed_two, expand) + thresholds
    active, slope = gelu_pair(expanded)
    grad = dot_t(grad_out, contract) * slope
    return active.astype(BF16), grad


def attention_block(normed_one, grad_out, allowed, position, inlet_t, offsets, outlet, heads, size):
    n = normed_one.shape[0]
    columns = inlet_t.shape[0]
    width = -(-columns // 128) * 128
    tables = rope_tables(position, heads, size, width)
    projected = dot_t(normed_one, inlet_t) + offsets
    if width > columns:
        projected = jnp.concatenate([projected, jnp.zeros((n, width - columns), F32)], axis=1)
    turned = turn(projected, tables, 1.0).astype(BF16)
    attended_grad = dot_t(grad_out, outlet).astype(BF16)
    attended, grads = [], []
    for head in range(heads):
        at = 3 * head * size
        query = turned[:, at : at + size]
        key = turned[:, at + size : at + 2 * size]
        value = turned[:, at + 2 * size : at + 3 * size]
        back = attended_grad[:, head * size : (head + 1) * size]
        scores = jnp.where(allowed, dot_t(query, key) * 0.125, -jnp.inf)
        raised = jnp.exp(scores - jnp.max(scores, axis=-1, keepdims=True))
        weight = raised * (1.0 / jnp.sum(raised, axis=-1, keepdims=True))
        softmax = weight.astype(BF16)
        attended.append(dot(softmax, value).astype(BF16))
        prob_grad = dot_t(back, value)
        delta = jnp.sum(weight * prob_grad, axis=-1, keepdims=True)
        score_grad = (weight * (prob_grad - delta)).astype(BF16)
        grads.append(dot(score_grad, key) * 0.125)
        grads.append(dot_rows(score_grad, query) * 0.125)
        grads.append(dot_rows(softmax, back))
    if width > columns:
        grads.append(jnp.zeros((n, width - columns), F32))
    inlet_full = turn(jnp.concatenate(grads, axis=1), tables, -1.0)
    return jnp.concatenate(attended, axis=1), inlet_full


def flat(ref):
    rows = [ref[i : i + 1, :] for i in range(ref.shape[0])]
    return jnp.concatenate(rows, axis=1) if len(rows) > 1 else rows[0]


def folded(value):
    size = value.shape[0]
    return value.reshape(size // 128, 128) if size % 128 == 0 else value.reshape(1, size)


def label_row(seg_ref):
    return flat(seg_ref).astype(F32)


def live_column(seg_row):
    down = jnp.broadcast_to(seg_row, (128, seg_row.shape[1])).T
    return jnp.where(down[:, :1] >= 0.0, 1.0, 0.0)


def gather_kernel(tok_ref, cot_ref, seg_any, out_ref, seg_ref, sem, seg_sem):
    n = tok_ref.shape[0]
    labels = pltpu.make_async_copy(seg_any, seg_ref, seg_sem)
    labels.start()

    @pl.when(core_bit() == 0)
    def _():
        pltpu.make_async_copy(tok_ref, out_ref.at[0:n], sem).start()

    @pl.when(core_bit() != 0)
    def _():
        pltpu.make_async_copy(cot_ref, out_ref.at[0:n], sem).start()

    width = out_ref.shape[1]
    labels.wait()
    row = label_row(seg_ref)
    row = jnp.concatenate([row, jnp.zeros((1, width - n), F32)], axis=1)
    out_ref[n : n + 8] = jnp.broadcast_to(row, (8, width)).astype(BF16)
    pltpu.make_async_copy(tok_ref, out_ref.at[0:n], sem).wait()


def own_kernel(
    heads, size, n_dp,
    tok_any, cot_any, seg_ref, gain_one_ref, shift_one_ref, gain_two_ref, shift_two_ref, offsets_ref, thr_ref,
    inlet_any, outlet_any, expand_any, contract_any,
    tok_ref, cot_ref, inlet_ref, outlet_ref, expand_ref, contract_ref,
    away_ref, keep_ref, active_ref, back_ref, attended_ref, inlet_back_ref, tile_away_ref, tile_keep_ref, one_ref, two_ref, out_ref,
    sems,
):
    copies = [
        pltpu.make_async_copy(a, b, sems.at[i])
        for i, (a, b) in enumerate(
            [(tok_any, tok_ref), (cot_any, cot_ref), (expand_any, expand_ref), (contract_any, contract_ref),
             (inlet_any, inlet_ref), (outlet_any, outlet_ref)]
        )
    ]
    for copy in copies:
        copy.start()
    seg_row = label_row(seg_ref)
    allowed, live, position = label_tables(seg_row)
    gain_one, shift_one = flat(gain_one_ref), flat(shift_one_ref)
    gain_two, shift_two = flat(gain_two_ref), flat(shift_two_ref)
    offsets = jnp.concatenate([offsets_ref[i : i + 1, :] for i in range(heads)], axis=1)
    thr = flat(thr_ref)
    copies[0].wait()
    scaled, inverse = norm_parts(tok_ref[...])
    normed_one = (scaled * gain_one + shift_one).astype(BF16)
    normed_two = (scaled * gain_two + shift_two).astype(BF16)
    copies[1].wait()
    grad_full = cot_ref[...].astype(F32) * live
    grad_out = grad_full.astype(BF16)
    put_left(normed_one, one_ref)
    put_left(normed_two, two_ref)
    put_left(grad_out, out_ref)
    copies[2].wait()
    copies[3].wait()
    active, expanded_grad = ffn_block(normed_two, grad_out, expand_ref[...], thr, contract_ref[...])
    expanded_back = expanded_grad.astype(BF16)
    copies[4].wait()
    copies[5].wait()
    attended, inlet_full = attention_block(
        normed_one, grad_out, allowed, position, inlet_ref[...], offsets, outlet_ref[...], heads, size
    )
    columns = inlet_ref.shape[0]
    inlet_back = inlet_full.astype(BF16)[:, :columns]
    active_ref[...] = active
    back_ref[...] = expanded_back
    attended_ref[...] = attended
    inlet_back_ref[...] = inlet_back
    branch = dot(attended, outlet_ref[...]) + dot(active, contract_ref[...])
    one_grad = dot(inlet_back, inlet_ref[...])
    two_grad = dot_t(expanded_back, expand_ref[...])
    lifted = one_grad * gain_one + two_grad * gain_two
    local = inverse * (
        lifted
        - jnp.mean(lifted, axis=-1, keepdims=True)
        - scaled * jnp.mean(lifted * scaled, axis=-1, keepdims=True)
    )
    core = core_bit()
    away_ref[...] = jnp.where(core == 0, local, branch).astype(BF16)
    keep_ref[...] = jnp.where(core == 0, branch, local)

    def total(field):
        return jnp.sum(field, axis=0, keepdims=True)

    everyone = jnp.concatenate(
        [total(one_grad * scaled), total(one_grad), total(two_grad * scaled), total(two_grad)], axis=0
    )
    bias = total(grad_full)
    hidden = total(expanded_grad)
    shares = total(inlet_full)
    block = tile_keep_ref.shape[2]
    third = 3 * size // n_dp
    per_dp = hidden.shape[1] // n_dp

    def tile(d):
        lanes = slice(d * block, (d + 1) * block)
        local = hidden[:, d * per_dp : (d + 1) * per_dp]
        if per_dp < block:
            local = jnp.concatenate([local, jnp.zeros((1, block - per_dp), F32)], axis=1)
        cut = [shares[:, h * 3 * size + d * third : h * 3 * size + (d + 1) * third] for h in range(heads)]
        if heads * third < block:
            cut.append(jnp.zeros((1, block - heads * third), F32))
        return jnp.concatenate(
            [everyone[:, lanes], bias[:, lanes], local, jnp.concatenate(cut, axis=1), jnp.zeros((1, block), F32)], axis=0
        )

    upper = bit_of(1) == 1
    for place, number in enumerate(rest_order(n_dp)):
        low, high = tile(number), tile(number + 1)
        tile_away_ref[place] = jnp.where(upper, low, high).astype(BF16)
        tile_keep_ref[place] = jnp.where(upper, high, low)


def bit_of(bit):
    return lax.axis_index("dp") // bit % 2


def core_bit():
    return lax.axis_index("tensor") % 2


def other_bits(dests, first):
    return [1 << i for i in range(12) if 1 << i < dests and 1 << i not in (2, first)]


def rest_order(dests):
    return list(range(0, dests, 2))


def dest_order(dests, first):
    bits = other_bits(dests, first)
    return [sum(bit for i, bit in enumerate(bits) if rest >> i & 1) for rest in range(1 << len(bits))]


def put_left(left, ref):
    ref[...] = left.T if ref.shape[0] != left.shape[0] else left


def left_shape(n, width, dests):
    return (width, n) if width // dests % 16 == 0 and width != n else (n, width)


def spread_rows(refs, dests, first):
    _, width = sorted(refs[0].shape)
    block = width // dests
    numbers = dest_order(dests, first)
    if refs[0].shape[0] == width:
        rows = []
        for flip in (1, 0):
            side = bit_of(first) if flip == 0 else 1 - bit_of(first)
            for number in numbers:
                start = pl.multiple_of((number + 2 * bit_of(2) + first * side) * block, 16)
                rows.append(jnp.concatenate([ref[pl.ds(start, block), :] for ref in refs], axis=1))
        return jnp.concatenate(rows, axis=0)
    half = len(numbers) * block
    row = lax.broadcasted_iota(jnp.int32, (2 * half, width), 0)
    col = lax.broadcasted_iota(jnp.int32, (2 * half, width), 1)
    kept = row >= half
    row = jnp.where(kept, row - half, row)
    side = jnp.where(kept, bit_of(first), 1 - bit_of(first))
    want = row + (2 * bit_of(2) + first * side) * block
    for place, number in enumerate(numbers):
        inside = (row >= place * block) & (row < (place + 1) * block)
        want = want + jnp.where(inside, (number - place) * block, 0)
    left = jnp.concatenate([ref[...] for ref in refs], axis=0)
    return dot_t(jnp.where(want == col, 1.0, 0.0).astype(BF16), left).astype(BF16)


def partner_inputs(got_ref, swap_ref, n):
    core = core_bit()
    got, swapped = got_ref[0:n], swap_ref[0:n]
    tok = jnp.where(core == 0, got, swapped)
    cot = jnp.where(core == 0, swapped, got)
    return tok, cot, got_ref[n : n + 1, :n].astype(F32)


def put_halves(product, send_ref, keep_ref):
    half = product.shape[0] // 2
    send_ref[...] = product[:half].astype(BF16)
    keep_ref[...] = product[half:]


def expand_kernel(
    dests, first,
    got_ref, swap_ref, two_ref, gain_ref, shift_ref, expand_ref, thr_ref, contract_ref, back_ref,
    send_ref, keep_ref, active_ref, grad_ref,
    left_ref,
):
    n = back_ref.shape[0]
    tok, cot, seg = partner_inputs(got_ref, swap_ref, n)
    scaled, _ = norm_parts(tok)
    normed = (scaled * flat(gain_ref) + flat(shift_ref)).astype(BF16)
    grad_out = (cot.astype(F32) * live_column(seg)).astype(BF16)
    grad_ref[...] = grad_out
    put_left(normed, left_ref)
    active, grad = ffn_block(normed, grad_out, expand_ref[...], flat(thr_ref), contract_ref[...])
    active_ref[...] = active
    right = jnp.concatenate([back_ref[...], grad.astype(BF16)], axis=0)
    put_halves(dot(spread_rows((two_ref, left_ref), dests, first), right), send_ref, keep_ref)


def contract_kernel(dests, grad_ref, out_ref, own_ref, active_ref, send_ref, keep_ref, left_ref):
    put_left(grad_ref[...], left_ref)
    right = jnp.concatenate([own_ref[...], active_ref[...]], axis=0)
    put_halves(dot(spread_rows((out_ref, left_ref), dests, 1), right), send_ref, keep_ref)


def attention_kernel(
    heads, size, dests,
    got_ref, swap_ref, grad_ref, gain_ref, shift_ref, inlet_ref, offsets_ref, outlet_ref, attended_ref, inlet_back_ref,
    one_ref, out_ref, near_ref,
    send_ref, keep_ref,
    left_ref,
):
    n = attended_ref.shape[0]
    tok, _, seg = partner_inputs(got_ref, swap_ref, n)
    allowed, _, position = label_tables(seg)
    offsets = jnp.concatenate([offsets_ref[i : i + 1, :] for i in range(heads)], axis=1)
    scaled, _ = norm_parts(tok)
    normed = (scaled * flat(gain_ref) + flat(shift_ref)).astype(BF16)
    put_left(normed, left_ref)
    attended, inlet_full = attention_block(
        normed, grad_ref[...], allowed, position, inlet_ref[...], offsets, outlet_ref[...], heads, size
    )
    inlet_back = inlet_full.astype(BF16)[:, : inlet_ref.shape[0]]
    right = jnp.concatenate([inlet_back_ref[...], inlet_back], axis=0)
    first = dot(spread_rows((one_ref, left_ref), dests, 1), right)
    right = jnp.concatenate([attended_ref[...], attended], axis=0)
    second = dot(spread_rows((out_ref, near_ref), dests, 1), right)
    put_halves(jnp.concatenate([first, second], axis=1), send_ref, keep_ref)


def halve_kernel(step, keep_ref, got_ref, send_ref, left_ref):
    bit = bit_of(step)
    for i in range(send_ref.shape[0]):
        away, stay = 2 * i + 1 - bit, 2 * i + bit
        send_ref[i] = (keep_ref[away] + got_ref[away].astype(F32)).astype(BF16)
        left_ref[i] = keep_ref[stay] + got_ref[stay].astype(F32)


def add_kernel(keep_ref, got_ref, out_ref):
    out_ref[...] = keep_ref[0] + got_ref[0].astype(F32)


def split_kernel(keep_ref, got_ref, inlet_ref, outlet_ref):
    total = keep_ref[0] + got_ref[0].astype(F32)
    columns = inlet_ref.shape[1]
    inlet_ref[...] = total[:, :columns]
    outlet_ref[...] = total[:, columns:].T


def part_kernel(keep_ref, got_ref, out_ref):
    out_ref[...] = (keep_ref[...].astype(F32) + got_ref[...].astype(F32)).astype(BF16)


def done_kernel(part_ref, got_ref, tok_ref, cot_ref, seg_ref, bias_ref, other_ref, out_ref):
    part = part_ref[...].astype(F32) + got_ref[...].astype(F32)
    shift = flat(bias_ref) + flat(other_ref)
    live = live_column(label_row(seg_ref))
    base = jnp.where(core_bit() == 0, tok_ref[...].astype(F32) + shift, cot_ref[...].astype(F32) * live)
    out_ref[...] = (base + part).astype(BF16)


def pair_kernel(own_ref, got_ref, mixed_ref, grad_ref):
    first = core_bit() == 0
    own, got = own_ref[...], got_ref[...]
    mixed_ref[...] = jnp.where(first, own, got)
    grad_ref[...] = jnp.where(first, got, own)


def small_kernel(heads, third, keep_ref, got_ref, norms_ref, bias_ref, thr_ref, offsets_ref):
    total = keep_ref[0] + got_ref[0].astype(F32)
    norms_ref[...] = total
    bias_ref[...] = total[4:5]
    thr_ref[...] = total[5:6, : thr_ref.shape[1]]
    for head in range(heads):
        offsets_ref[head : head + 1] = total[6:7, head * third : (head + 1) * third]


def rows_kernel(own_ref, got_ref, out_ref):
    out_ref[...] = (own_ref[...] + got_ref[...])[: out_ref.shape[0]]


def call(kernel, outs, args, flops=0, scratch=(), limit=VMEM_LIMIT, places="", results=""):
    kinds = {"v": pl.BlockSpec(memory_space=pltpu.VMEM), "a": pl.BlockSpec(memory_space=pltpu.HBM), "d": pl.BlockSpec()}
    places = places or "v" * len(args)
    results = results or "v" * len(outs)
    moved = sum(math.prod(s) * jnp.dtype(t).itemsize for s, t in outs)
    moved += sum(math.prod(a.shape) * a.dtype.itemsize for a in args)
    args = [pltpu.with_memory_space_constraint(a, pltpu.HBM) if k == "a" else a for a, k in zip(args, places)]
    return pl.pallas_call(
        kernel,
        out_shape=[jax.ShapeDtypeStruct(shape, dtype) for shape, dtype in outs],
        in_specs=[kinds[k] for k in places],
        out_specs=[kinds[k] for k in results],
        scratch_shapes=list(scratch),
        compiler_params=pltpu.CompilerParams(vmem_limit_bytes=limit),
        cost_estimate=pl.CostEstimate(flops=int(flops), bytes_accessed=moved, transcendentals=0),
    )(*args)


def swap(value, axis, count, bit):
    return lax.ppermute(value, axis, [(i, i ^ bit) for i in range(count)])


def step(n_dp, n_tensor, tokens, segments, first_gain, first_shift, second_gain, second_shift, inlet, offsets,
         outlet, outlet_bias, expand, thresholds, contract, contract_bias, cotangent):
    n, width = tokens.shape
    heads, size = offsets.shape[0], offsets.shape[1] // 3
    units = expand.shape[1]
    columns = inlet.shape[1]
    mine = outlet.shape[0]
    block = width // n_dp
    seg = folded(segments)
    gain_one, shift_one, gain_two, shift_two = map(folded, (first_gain, first_shift, second_gain, second_shift))
    thr = folded(thresholds)

    turned = left_shape(n, width, n_dp)

    payload, = call(
        gather_kernel, [((n + 8, width), BF16)], [tokens, cotangent, seg],
        scratch=[pltpu.VMEM(seg.shape, seg.dtype), pltpu.SemaphoreType.DMA, pltpu.SemaphoreType.DMA], places="aaa",
    )
    got = swap(payload, "dp", n_dp, 2)
    other = swap(got, "tensor", n_tensor, 1)

    (tok, cot, inlet_v, outlet_v, expand_v, contract_v, away, keep, active, back, attended, inlet_back, tile_away, tile_keep,
     one_t, two_t, out_t) = call(
        functools.partial(own_kernel, heads, size, n_dp),
        [(tokens.shape, BF16), (cotangent.shape, BF16), ((columns, width), BF16), (outlet.shape, BF16), (expand.shape, BF16),
         (contract.shape, BF16), ((n, width), BF16), ((n, width), F32), ((n, units), BF16), ((n, units), BF16),
         ((n, mine), BF16), ((n, columns), BF16), ((n_dp // 2, 8, block), BF16), ((n_dp // 2, 8, block), F32),
         (turned, BF16), (turned, BF16), (turned, BF16)],
        [tokens, cotangent, seg, gain_one, shift_one, gain_two, shift_two, offsets, thr, inlet.T, outlet, expand, contract],
        flops=6e9, scratch=[pltpu.SemaphoreType.DMA((6,))], places="aavvvvvvvaaaa",
    )
    half = n_dp // 4 * block
    left = [pltpu.VMEM(turned, BF16)]

    far_first = 4 if n_dp > 4 else 1
    expand_send, expand_keep, active_near, grad_near = call(
        functools.partial(expand_kernel, n_dp, far_first),
        [((half, units), BF16), ((half, units), F32), ((n, units), BF16), ((n, width), BF16)],
        [got, other, two_t, gain_two, shift_two, expand_v, thr, contract_v, back],
        flops=3e9, scratch=left,
    )
    expand_got = swap(expand_send, "dp", n_dp, far_first)
    contract_send, contract_keep, near_t = call(
        functools.partial(contract_kernel, n_dp),
        [((half, units), BF16), ((half, units), F32), (turned, BF16)],
        [grad_near, out_t, active, active_near],
        flops=1e9,
    )
    contract_got = swap(contract_send, "dp", n_dp, 1)
    tail_send, tail_keep = call(
        functools.partial(attention_kernel, heads, size, n_dp),
        [((half, columns + mine), BF16), ((half, columns + mine), F32)],
        [got, other, grad_near, gain_one, shift_one, inlet_v, offsets, outlet_v, attended, inlet_back, one_t, out_t, near_t],
        flops=5e9, scratch=left,
    )
    tail_got = swap(tail_send, "dp", n_dp, 1)

    part = keep
    near = swap(away, "tensor", n_tensor, 1)
    part, = call(part_kernel, [((n, width), BF16)], [keep, near], flops=1e6)
    bit = 2
    while 2 * bit < n_tensor:
        part, = call(part_kernel, [((n, width), BF16)], [part, swap(part, "tensor", n_tensor, bit)])
        bit *= 2
    far = swap(part, "tensor", n_tensor, bit)
    done, = call(
        done_kernel, [((n, width), BF16)],
        [part, far, tok, cot, seg, folded(outlet_bias), folded(contract_bias)], flops=1e6,
    )
    paired = swap(done, "tensor", n_tensor, 1)
    mixed, input_grad = call(pair_kernel, [((n, width), BF16)] * 2, [done, paired], results="dd")

    def halve(bit, kept, arrived):
        shape = (kept.shape[0] // 2,) + kept.shape[1:]
        return call(functools.partial(halve_kernel, bit), [(shape, BF16), (shape, F32)], [kept, arrived], flops=1e6)

    def reduce(kept, arrived, first):
        kept = kept.reshape(-1, block, kept.shape[1])
        arrived = arrived.reshape(kept.shape)
        for bit in other_bits(n_dp, first):
            away, kept = halve(bit, kept, arrived)
            arrived = swap(away, "dp", n_dp, bit)
        return [kept, arrived]

    kept, arrived = tile_keep, swap(tile_away, "dp", n_dp, 1)
    bit = 2
    while bit < n_dp:
        away, kept = halve(bit, kept, arrived)
        arrived = swap(away, "dp", n_dp, bit)
        bit *= 2
    third = offsets.shape[1] // n_dp
    norms, bias_grad, thr_grad, offsets_grad = call(
        functools.partial(small_kernel, heads, third),
        [((8, block), F32), ((1, block), F32), ((1, units // n_dp), F32), ((heads, third), F32)], [kept, arrived],
        results="vddd",
    )
    bit = 1
    while 2 * bit < n_tensor:
        norms, = call(rows_kernel, [((8, block), F32)], [norms, swap(norms, "tensor", n_tensor, bit)])
        bit *= 2
    norm_grads, = call(rows_kernel, [((4, block), F32)], [norms, swap(norms, "tensor", n_tensor, bit)], results="d")

    expand_grad, = call(add_kernel, [((block, units), F32)], reduce(expand_keep, expand_got, far_first), results="d")
    contract_grad, = call(add_kernel, [((block, units), F32)], reduce(contract_keep, contract_got, 1), results="d")
    inlet_grad, outlet_grad = call(
        split_kernel, [((block, columns), F32), ((mine, block), F32)],
        reduce(tail_keep, tail_got, 1), results="dd",
    )
    return (
        mixed, input_grad, inlet_grad, offsets_grad, outlet_grad, expand_grad, thr_grad, contract_grad.T,
        bias_grad.reshape(block), norm_grads,
    )


def solution(mesh):
    placed = (
        P("dp", None), P("dp"), P(), P(), P(), P(), P(None, "tensor"), P("tensor", None), P("tensor", None),
        P(), P(None, "tensor"), P("tensor"), P("tensor", None), P(), P("dp", None),
    )
    return jax.shard_map(
        functools.partial(step, mesh.shape["dp"], mesh.shape["tensor"]),
        mesh=mesh,
        in_specs=placed,
        out_specs=(
            P("dp", None), P("dp", None), P("dp", "tensor"), P("tensor", "dp"), P("tensor", "dp"),
            P("dp", "tensor"), P("tensor", "dp"), P("tensor", "dp"), P("dp"), P(None, "dp"),
        ),
        check_vma=False,
    )
```

```python
import functools
import math

import jax
import jax.numpy as jnp
from jax import lax
from jax.experimental import pallas as pl
from jax.experimental.pallas import tpu as pltpu
from jax.sharding import PartitionSpec as P


ROT = 16
EPS = 1e-05
F32 = jnp.float32
BF16 = jnp.bfloat16
MIB = 1024 * 1024
VMEM_LIMIT = 32 * MIB


def dot(a, b):
    return jnp.dot(a, b, preferred_element_type=F32)


def dot_t(a, b):
    return lax.dot_general(a, b, (((1,), (1,)), ((), ())), preferred_element_type=F32)


def dot_rows(a, b):
    return lax.dot_general(a, b, (((0,), (0,)), ((), ())), preferred_element_type=F32)


def norm_parts(tok):
    x = tok.astype(F32)
    center = x - jnp.mean(x, axis=-1, keepdims=True)
    inverse = lax.rsqrt(jnp.mean(center * center, axis=-1, keepdims=True) + EPS)
    return center * inverse, inverse


def label_tables(seg_row):
    n = seg_row.shape[1]
    across = jnp.broadcast_to(seg_row, (n, n))
    down = across.T
    row = lax.broadcasted_iota(jnp.int32, (n, n), 0)
    col = lax.broadcasted_iota(jnp.int32, (n, n), 1)
    same = across == down
    allowed = same & (col <= row)
    position = jnp.sum(jnp.where(same & (row <= col), 1.0, 0.0), axis=0, keepdims=True) - 1.0
    live = jnp.where(down[:, :1] >= 0.0, 1.0, 0.0)
    return allowed, live, position


def rope_tables(position, heads, size, width):
    half = ROT // 2
    index = lax.broadcasted_iota(jnp.int32, (half, 1), 0).astype(F32)
    angle = jnp.exp(index * (-2.0 * math.log(10000.0) / ROT)) * position
    cosine = jnp.concatenate([jnp.cos(angle)] * (128 // half), axis=0).T
    sine = jnp.concatenate([jnp.sin(angle)] * (128 // half), axis=0).T
    lane = lax.broadcasted_iota(jnp.int32, (1, width), 1)
    part, dim = lane // size, lane % size
    value = part >= 3 * heads
    for head in range(heads):
        value = value | (part == 3 * head + 2)
    turned = jnp.logical_not(value) & (dim < ROT)
    low = turned & (dim < half)
    high = turned & (dim >= half)
    blocks = width // 128
    cosine = jnp.concatenate([cosine] * blocks, axis=1)
    sine = jnp.concatenate([sine] * blocks, axis=1)
    return (
        jnp.where(turned, cosine, 1.0),
        jnp.where(low, sine, 0.0),
        jnp.where(high, sine, 0.0),
    )


def turn(field, tables, sign):
    cosine, low, high = tables
    width = field.shape[1]
    ahead = pltpu.roll(field, width - ROT // 2, 1)
    behind = pltpu.roll(field, ROT // 2, 1)
    return field * cosine + sign * (behind * high - ahead * low)


def gelu_pair(expanded):
    cumulative = 0.5 * (1.0 + lax.erf(expanded * (1.0 / math.sqrt(2.0))))
    density = jnp.exp(-0.5 * expanded * expanded) * (1.0 / math.sqrt(2.0 * math.pi))
    return expanded * cumulative, cumulative + expanded * density


def ffn_block(normed_two, grad_out, expand, thresholds, contract):
    expanded = dot(normed_two, expand) + thresholds
    active, slope = gelu_pair(expanded)
    grad = dot_t(grad_out, contract) * slope
    return active.astype(BF16), grad


def attention_block(normed_one, grad_out, allowed, position, inlet_t, offsets, outlet, heads, size):
    n = normed_one.shape[0]
    columns = inlet_t.shape[0]
    width = -(-columns // 128) * 128
    tables = rope_tables(position, heads, size, width)
    projected = dot_t(normed_one, inlet_t) + offsets
    if width > columns:
        projected = jnp.concatenate([projected, jnp.zeros((n, width - columns), F32)], axis=1)
    turned = turn(projected, tables, 1.0).astype(BF16)
    attended_grad = dot_t(grad_out, outlet).astype(BF16)
    attended, grads = [], []
    for head in range(heads):
        at = 3 * head * size
        query = turned[:, at : at + size]
        key = turned[:, at + size : at + 2 * size]
        value = turned[:, at + 2 * size : at + 3 * size]
        back = attended_grad[:, head * size : (head + 1) * size]
        scores = jnp.where(allowed, dot_t(query, key) * 0.125, -jnp.inf)
        raised = jnp.exp(scores - jnp.max(scores, axis=-1, keepdims=True))
        weight = raised * (1.0 / jnp.sum(raised, axis=-1, keepdims=True))
        softmax = weight.astype(BF16)
        attended.append(dot(softmax, value).astype(BF16))
        prob_grad = dot_t(back, value)
        delta = jnp.sum(weight * prob_grad, axis=-1, keepdims=True)
        score_grad = (weight * (prob_grad - delta)).astype(BF16)
        grads.append(dot(score_grad, key) * 0.125)
        grads.append(dot_rows(score_grad, query) * 0.125)
        grads.append(dot_rows(softmax, back))
    if width > columns:
        grads.append(jnp.zeros((n, width - columns), F32))
    inlet_full = turn(jnp.concatenate(grads, axis=1), tables, -1.0)
    return jnp.concatenate(attended, axis=1), inlet_full


def flat(ref):
    rows = [ref[i : i + 1, :] for i in range(ref.shape[0])]
    return jnp.concatenate(rows, axis=1) if len(rows) > 1 else rows[0]


def folded(value):
    size = value.shape[0]
    return value.reshape(size // 128, 128) if size % 128 == 0 else value.reshape(1, size)


def label_row(seg_ref):
    return flat(seg_ref).astype(F32)


def live_column(seg_row):
    down = jnp.broadcast_to(seg_row, (128, seg_row.shape[1])).T
    return jnp.where(down[:, :1] >= 0.0, 1.0, 0.0)


def gather_kernel(tok_ref, cot_ref, seg_any, out_ref, seg_ref, sem, seg_sem):
    n = tok_ref.shape[0]
    labels = pltpu.make_async_copy(seg_any, seg_ref, seg_sem)
    labels.start()

    @pl.when(core_bit() == 0)
    def _():
        pltpu.make_async_copy(tok_ref, out_ref.at[0:n], sem).start()

    @pl.when(core_bit() != 0)
    def _():
        pltpu.make_async_copy(cot_ref, out_ref.at[0:n], sem).start()

    width = out_ref.shape[1]
    labels.wait()
    row = label_row(seg_ref)
    row = jnp.concatenate([row, jnp.zeros((1, width - n), F32)], axis=1)
    out_ref[n : n + 8] = jnp.broadcast_to(row, (8, width)).astype(BF16)
    pltpu.make_async_copy(tok_ref, out_ref.at[0:n], sem).wait()


def own_kernel(
    heads, size, n_dp,
    tok_any, cot_any, seg_ref, gain_one_ref, shift_one_ref, gain_two_ref, shift_two_ref, offsets_ref, thr_ref,
    inlet_any, outlet_any, expand_any, contract_any,
    tok_ref, cot_ref, inlet_ref, outlet_ref, expand_ref, contract_ref,
    away_ref, keep_ref, active_ref, back_ref, attended_ref, inlet_back_ref, tile_away_ref, tile_keep_ref, one_ref, two_ref, out_ref,
    sems,
):
    copies = [
        pltpu.make_async_copy(a, b, sems.at[i])
        for i, (a, b) in enumerate(
            [(tok_any, tok_ref), (cot_any, cot_ref), (expand_any, expand_ref), (contract_any, contract_ref),
             (inlet_any, inlet_ref), (outlet_any, outlet_ref)]
        )
    ]
    for copy in copies:
        copy.start()
    seg_row = label_row(seg_ref)
    allowed, live, position = label_tables(seg_row)
    gain_one, shift_one = flat(gain_one_ref), flat(shift_one_ref)
    gain_two, shift_two = flat(gain_two_ref), flat(shift_two_ref)
    offsets = jnp.concatenate([offsets_ref[i : i + 1, :] for i in range(heads)], axis=1)
    thr = flat(thr_ref)
    copies[0].wait()
    scaled, inverse = norm_parts(tok_ref[...])
    normed_one = (scaled * gain_one + shift_one).astype(BF16)
    normed_two = (scaled * gain_two + shift_two).astype(BF16)
    copies[1].wait()
    grad_full = cot_ref[...].astype(F32) * live
    grad_out = grad_full.astype(BF16)
    put_left(normed_one, one_ref)
    put_left(normed_two, two_ref)
    put_left(grad_out, out_ref)
    copies[2].wait()
    copies[3].wait()
    active, expanded_grad = ffn_block(normed_two, grad_out, expand_ref[...], thr, contract_ref[...])
    expanded_back = expanded_grad.astype(BF16)
    copies[4].wait()
    copies[5].wait()
    attended, inlet_full = attention_block(
        normed_one, grad_out, allowed, position, inlet_ref[...], offsets, outlet_ref[...], heads, size
    )
    columns = inlet_ref.shape[0]
    inlet_back = inlet_full.astype(BF16)[:, :columns]
    active_ref[...] = active
    back_ref[...] = expanded_back
    attended_ref[...] = attended
    inlet_back_ref[...] = inlet_back
    branch = dot(attended, outlet_ref[...]) + dot(active, contract_ref[...])
    one_grad = dot(inlet_back, inlet_ref[...])
    two_grad = dot_t(expanded_back, expand_ref[...])
    lifted = one_grad * gain_one + two_grad * gain_two
    local = inverse * (
        lifted
        - jnp.mean(lifted, axis=-1, keepdims=True)
        - scaled * jnp.mean(lifted * scaled, axis=-1, keepdims=True)
    )
    core = core_bit()
    away_ref[...] = jnp.where(core == 0, local, branch).astype(BF16)
    keep_ref[...] = jnp.where(core == 0, branch, local)

    def total(field):
        return jnp.sum(field, axis=0, keepdims=True)

    everyone = jnp.concatenate(
        [total(one_grad * scaled), total(one_grad), total(two_grad * scaled), total(two_grad)], axis=0
    )
    bias = total(grad_full)
    hidden = total(expanded_grad)
    shares = total(inlet_full)
    block = tile_keep_ref.shape[2]
    third = 3 * size // n_dp
    per_dp = hidden.shape[1] // n_dp

    def tile(d):
        lanes = slice(d * block, (d + 1) * block)
        local = hidden[:, d * per_dp : (d + 1) * per_dp]
        if per_dp < block:
            local = jnp.concatenate([local, jnp.zeros((1, block - per_dp), F32)], axis=1)
        cut = [shares[:, h * 3 * size + d * third : h * 3 * size + (d + 1) * third] for h in range(heads)]
        if heads * third < block:
            cut.append(jnp.zeros((1, block - heads * third), F32))
        return jnp.concatenate(
            [everyone[:, lanes], bias[:, lanes], local, jnp.concatenate(cut, axis=1), jnp.zeros((1, block), F32)], axis=0
        )

    upper = bit_of(1) == 1
    for place, number in enumerate(rest_order(n_dp)):
        low, high = tile(number), tile(number + 1)
        tile_away_ref[place] = jnp.where(upper, low, high).astype(BF16)
        tile_keep_ref[place] = jnp.where(upper, high, low)


def bit_of(bit):
    return lax.axis_index("dp") // bit % 2


def core_bit():
    return lax.axis_index("tensor") % 2


def other_bits(dests, first):
    return [1 << i for i in range(12) if 1 << i < dests and 1 << i not in (2, first)]


def rest_order(dests):
    return list(range(0, dests, 2))


def dest_order(dests, first):
    bits = other_bits(dests, first)
    return [sum(bit for i, bit in enumerate(bits) if rest >> i & 1) for rest in range(1 << len(bits))]


def put_left(left, ref):
    ref[...] = left.T if ref.shape[0] != left.shape[0] else left


def left_shape(n, width, dests):
    return (width, n) if width // dests % 16 == 0 and width != n else (n, width)


def spread_rows(refs, dests, first):
    _, width = sorted(refs[0].shape)
    block = width // dests
    numbers = dest_order(dests, first)
    if refs[0].shape[0] == width:
        rows = []
        for flip in (1, 0):
            side = bit_of(first) if flip == 0 else 1 - bit_of(first)
            for number in numbers:
                start = pl.multiple_of((number + 2 * bit_of(2) + first * side) * block, 16)
                rows.append(jnp.concatenate([ref[pl.ds(start, block), :] for ref in refs], axis=1))
        return jnp.concatenate(rows, axis=0)
    half = len(numbers) * block
    row = lax.broadcasted_iota(jnp.int32, (2 * half, width), 0)
    col = lax.broadcasted_iota(jnp.int32, (2 * half, width), 1)
    kept = row >= half
    row = jnp.where(kept, row - half, row)
    side = jnp.where(kept, bit_of(first), 1 - bit_of(first))
    want = row + (2 * bit_of(2) + first * side) * block
    for place, number in enumerate(numbers):
        inside = (row >= place * block) & (row < (place + 1) * block)
        want = want + jnp.where(inside, (number - place) * block, 0)
    left = jnp.concatenate([ref[...] for ref in refs], axis=0)
    return dot_t(jnp.where(want == col, 1.0, 0.0).astype(BF16), left).astype(BF16)


def partner_inputs(got_ref, swap_ref, n):
    core = core_bit()
    got, swapped = got_ref[0:n], swap_ref[0:n]
    tok = jnp.where(core == 0, got, swapped)
    cot = jnp.where(core == 0, swapped, got)
    return tok, cot, got_ref[n : n + 1, :n].astype(F32)


def put_halves(product, send_ref, keep_ref):
    half = product.shape[0] // 2
    send_ref[...] = product[:half].astype(BF16)
    keep_ref[...] = product[half:]


def expand_kernel(
    dests, first,
    got_ref, swap_ref, two_ref, gain_ref, shift_ref, expand_ref, thr_ref, contract_ref, back_ref,
    send_ref, keep_ref, active_ref, grad_ref,
    left_ref,
):
    n = back_ref.shape[0]
    tok, cot, seg = partner_inputs(got_ref, swap_ref, n)
    scaled, _ = norm_parts(tok)
    normed = (scaled * flat(gain_ref) + flat(shift_ref)).astype(BF16)
    grad_out = (cot.astype(F32) * live_column(seg)).astype(BF16)
    grad_ref[...] = grad_out
    put_left(normed, left_ref)
    active, grad = ffn_block(normed, grad_out, expand_ref[...], flat(thr_ref), contract_ref[...])
    active_ref[...] = active
    right = jnp.concatenate([back_ref[...], grad.astype(BF16)], axis=0)
    put_halves(dot(spread_rows((two_ref, left_ref), dests, first), right), send_ref, keep_ref)


def contract_kernel(dests, grad_ref, out_ref, own_ref, active_ref, send_ref, keep_ref, left_ref):
    put_left(grad_ref[...], left_ref)
    right = jnp.concatenate([own_ref[...], active_ref[...]], axis=0)
    put_halves(dot(spread_rows((out_ref, left_ref), dests, 1), right), send_ref, keep_ref)


def attention_kernel(
    heads, size, dests,
    got_ref, swap_ref, grad_ref, gain_ref, shift_ref, inlet_ref, offsets_ref, outlet_ref, attended_ref, inlet_back_ref,
    one_ref, out_ref, near_ref,
    send_ref, keep_ref,
    left_ref,
):
    n = attended_ref.shape[0]
    tok, _, seg = partner_inputs(got_ref, swap_ref, n)
    allowed, _, position = label_tables(seg)
    offsets = jnp.concatenate([offsets_ref[i : i + 1, :] for i in range(heads)], axis=1)
    scaled, _ = norm_parts(tok)
    normed = (scaled * flat(gain_ref) + flat(shift_ref)).astype(BF16)
    put_left(normed, left_ref)
    attended, inlet_full = attention_block(
        normed, grad_ref[...], allowed, position, inlet_ref[...], offsets, outlet_ref[...], heads, size
    )
    inlet_back = inlet_full.astype(BF16)[:, : inlet_ref.shape[0]]
    right = jnp.concatenate([inlet_back_ref[...], inlet_back], axis=0)
    first = dot(spread_rows((one_ref, left_ref), dests, 1), right)
    right = jnp.concatenate([attended_ref[...], attended], axis=0)
    second = dot(spread_rows((out_ref, near_ref), dests, 1), right)
    put_halves(jnp.concatenate([first, second], axis=1), send_ref, keep_ref)


def halve_kernel(step, keep_ref, got_ref, send_ref, left_ref):
    bit = bit_of(step)
    for i in range(send_ref.shape[0]):
        away, stay = 2 * i + 1 - bit, 2 * i + bit
        send_ref[i] = (keep_ref[away] + got_ref[away].astype(F32)).astype(BF16)
        left_ref[i] = keep_ref[stay] + got_ref[stay].astype(F32)


def add_kernel(keep_ref, got_ref, out_ref):
    out_ref[...] = keep_ref[0] + got_ref[0].astype(F32)


def split_kernel(
    heads, third, keep_ref, got_ref, small_ref, norms_ref, far_ref,
    inlet_ref, outlet_ref, norm_ref, bias_ref, thr_ref, offsets_ref,
):
    total = keep_ref[0] + got_ref[0].astype(F32)
    columns = inlet_ref.shape[1]
    inlet_ref[...] = total[:, :columns]
    outlet_ref[...] = total[:, columns:].T
    norm_ref[...] = (norms_ref[...] + far_ref[...])[:4]
    small = small_ref[...]
    bias_ref[...] = small[4:5]
    thr_ref[...] = small[5:6, : thr_ref.shape[1]]
    for head in range(heads):
        offsets_ref[head : head + 1] = small[6:7, head * third : (head + 1) * third]


def part_kernel(keep_ref, got_ref, out_ref):
    out_ref[...] = (keep_ref[...].astype(F32) + got_ref[...].astype(F32)).astype(BF16)


def done_kernel(part_ref, got_ref, tok_ref, cot_ref, seg_ref, bias_ref, other_ref, out_ref):
    part = part_ref[...].astype(F32) + got_ref[...].astype(F32)
    shift = flat(bias_ref) + flat(other_ref)
    live = live_column(label_row(seg_ref))
    base = jnp.where(core_bit() == 0, tok_ref[...].astype(F32) + shift, cot_ref[...].astype(F32) * live)
    out_ref[...] = (base + part).astype(BF16)


def ends_kernel(
    own_ref, got_ref, keep_c_ref, got_c_ref, keep_e_ref, got_e_ref, mixed_ref, grad_ref, contract_ref, expand_ref
):
    first = core_bit() == 0
    own, got = own_ref[...], got_ref[...]
    mixed_ref[...] = jnp.where(first, own, got)
    grad_ref[...] = jnp.where(first, got, own)
    contract_ref[...] = keep_c_ref[0] + got_c_ref[0].astype(F32)
    expand_ref[...] = keep_e_ref[0] + got_e_ref[0].astype(F32)


def rows_kernel(own_ref, got_ref, out_ref):
    out_ref[...] = own_ref[...] + got_ref[...]


def call(kernel, outs, args, flops=0, scratch=(), limit=VMEM_LIMIT, places="", results=""):
    kinds = {"v": pl.BlockSpec(memory_space=pltpu.VMEM), "a": pl.BlockSpec(memory_space=pltpu.HBM), "d": pl.BlockSpec()}
    places = places or "v" * len(args)
    results = results or "v" * len(outs)
    moved = sum(math.prod(s) * jnp.dtype(t).itemsize for s, t in outs)
    moved += sum(math.prod(a.shape) * a.dtype.itemsize for a in args)
    args = [pltpu.with_memory_space_constraint(a, pltpu.HBM) if k == "a" else a for a, k in zip(args, places)]
    return pl.pallas_call(
        kernel,
        out_shape=[jax.ShapeDtypeStruct(shape, dtype) for shape, dtype in outs],
        in_specs=[kinds[k] for k in places],
        out_specs=[kinds[k] for k in results],
        scratch_shapes=list(scratch),
        compiler_params=pltpu.CompilerParams(vmem_limit_bytes=limit),
        cost_estimate=pl.CostEstimate(flops=int(flops), bytes_accessed=moved, transcendentals=0),
    )(*args)


def swap(value, axis, count, bit):
    return lax.ppermute(value, axis, [(i, i ^ bit) for i in range(count)])


def step(n_dp, n_tensor, tokens, segments, first_gain, first_shift, second_gain, second_shift, inlet, offsets,
         outlet, outlet_bias, expand, thresholds, contract, contract_bias, cotangent):
    n, width = tokens.shape
    heads, size = offsets.shape[0], offsets.shape[1] // 3
    units = expand.shape[1]
    columns = inlet.shape[1]
    mine = outlet.shape[0]
    block = width // n_dp
    seg = folded(segments)
    gain_one, shift_one, gain_two, shift_two = map(folded, (first_gain, first_shift, second_gain, second_shift))
    thr = folded(thresholds)

    turned = left_shape(n, width, n_dp)

    payload, = call(
        gather_kernel, [((n + 8, width), BF16)], [tokens, cotangent, seg],
        scratch=[pltpu.VMEM(seg.shape, seg.dtype), pltpu.SemaphoreType.DMA, pltpu.SemaphoreType.DMA], places="aaa",
    )
    got = swap(payload, "dp", n_dp, 2)
    other = swap(got, "tensor", n_tensor, 1)

    (tok, cot, inlet_v, outlet_v, expand_v, contract_v, away, keep, active, back, attended, inlet_back, tile_away, tile_keep,
     one_t, two_t, out_t) = call(
        functools.partial(own_kernel, heads, size, n_dp),
        [(tokens.shape, BF16), (cotangent.shape, BF16), ((columns, width), BF16), (outlet.shape, BF16), (expand.shape, BF16),
         (contract.shape, BF16), ((n, width), BF16), ((n, width), F32), ((n, units), BF16), ((n, units), BF16),
         ((n, mine), BF16), ((n, columns), BF16), ((n_dp // 2, 8, block), BF16), ((n_dp // 2, 8, block), F32),
         (turned, BF16), (turned, BF16), (turned, BF16)],
        [tokens, cotangent, seg, gain_one, shift_one, gain_two, shift_two, offsets, thr, inlet.T, outlet, expand, contract],
        flops=6e9, scratch=[pltpu.SemaphoreType.DMA((6,))], places="aavvvvvvvaaaa",
    )
    half = n_dp // 4 * block
    left = [pltpu.VMEM(turned, BF16)]

    far_first = 4 if n_dp > 4 else 1
    expand_send, expand_keep, active_near, grad_near = call(
        functools.partial(expand_kernel, n_dp, far_first),
        [((half, units), BF16), ((half, units), F32), ((n, units), BF16), ((n, width), BF16)],
        [got, other, two_t, gain_two, shift_two, expand_v, thr, contract_v, back],
        flops=3e9, scratch=left,
    )
    expand_got = swap(expand_send, "dp", n_dp, far_first)
    contract_send, contract_keep, near_t = call(
        functools.partial(contract_kernel, n_dp),
        [((half, units), BF16), ((half, units), F32), (turned, BF16)],
        [grad_near, out_t, active, active_near],
        flops=1e9,
    )
    contract_got = swap(contract_send, "dp", n_dp, 1)
    tail_send, tail_keep = call(
        functools.partial(attention_kernel, heads, size, n_dp),
        [((half, columns + mine), BF16), ((half, columns + mine), F32)],
        [got, other, grad_near, gain_one, shift_one, inlet_v, offsets, outlet_v, attended, inlet_back, one_t, out_t, near_t],
        flops=5e9, scratch=left,
    )
    tail_got = swap(tail_send, "dp", n_dp, 1)

    part = keep
    near = swap(away, "tensor", n_tensor, 1)
    part, = call(part_kernel, [((n, width), BF16)], [keep, near], flops=1e6)
    bit = 2
    while 2 * bit < n_tensor:
        part, = call(part_kernel, [((n, width), BF16)], [part, swap(part, "tensor", n_tensor, bit)])
        bit *= 2
    far = swap(part, "tensor", n_tensor, bit)
    done, = call(
        done_kernel, [((n, width), BF16)],
        [part, far, tok, cot, seg, folded(outlet_bias), folded(contract_bias)], flops=1e6,
    )
    paired = swap(done, "tensor", n_tensor, 1)

    def halve(bit, kept, arrived):
        shape = (kept.shape[0] // 2,) + kept.shape[1:]
        return call(functools.partial(halve_kernel, bit), [(shape, BF16), (shape, F32)], [kept, arrived], flops=1e6)

    def reduce(kept, arrived, first):
        kept = kept.reshape(-1, block, kept.shape[1])
        arrived = arrived.reshape(kept.shape)
        for bit in other_bits(n_dp, first):
            away, kept = halve(bit, kept, arrived)
            arrived = swap(away, "dp", n_dp, bit)
        return [kept, arrived]

    kept, arrived = tile_keep, swap(tile_away, "dp", n_dp, 1)
    bit = 2
    while bit < n_dp:
        away, kept = halve(bit, kept, arrived)
        arrived = swap(away, "dp", n_dp, bit)
        bit *= 2
    third = offsets.shape[1] // n_dp
    small, = call(add_kernel, [((8, block), F32)], [kept, arrived])
    norms = small
    bit = 1
    while 2 * bit < n_tensor:
        norms, = call(rows_kernel, [((8, block), F32)], [norms, swap(norms, "tensor", n_tensor, bit)])
        bit *= 2
    far_norms = swap(norms, "tensor", n_tensor, bit)

    contract_parts = reduce(contract_keep, contract_got, 1)
    expand_parts = reduce(expand_keep, expand_got, far_first)
    mixed, input_grad, contract_grad, expand_grad = call(
        ends_kernel, [((n, width), BF16), ((n, width), BF16), ((block, units), F32), ((block, units), F32)],
        [done, paired] + contract_parts + expand_parts, results="dddd",
    )
    inlet_grad, outlet_grad, norm_grads, bias_grad, thr_grad, offsets_grad = call(
        functools.partial(split_kernel, heads, third),
        [((block, columns), F32), ((mine, block), F32), ((4, block), F32), ((1, block), F32), ((1, units // n_dp), F32),
         ((heads, third), F32)],
        reduce(tail_keep, tail_got, 1) + [small, norms, far_norms], results="dddddd",
    )
    return (
        mixed, input_grad, inlet_grad, offsets_grad, outlet_grad, expand_grad, thr_grad, contract_grad.T,
        bias_grad.reshape(block), norm_grads,
    )


def solution(mesh):
    placed = (
        P("dp", None), P("dp"), P(), P(), P(), P(), P(None, "tensor"), P("tensor", None), P("tensor", None),
        P(), P(None, "tensor"), P("tensor"), P("tensor", None), P(), P("dp", None),
    )
    return jax.shard_map(
        functools.partial(step, mesh.shape["dp"], mesh.shape["tensor"]),
        mesh=mesh,
        in_specs=placed,
        out_specs=(
            P("dp", None), P("dp", None), P("dp", "tensor"), P("tensor", "dp"), P("tensor", "dp"),
            P("dp", "tensor"), P("tensor", "dp"), P("tensor", "dp"), P("dp"), P(None, "dp"),
        ),
        check_vma=False,
    )
```
